128 devices in a mesh: row: 8 (over y_lo, z), col: 16 (over x, y_hi, core).
Axes of the slice: x: 4, y: 4 (y_hi: 2, y_lo: 2; y = y_hi * 2 + y_lo), z: 4, core: 2. Of those that a mesh axis runs over, the one named last changes fastest.
Arguments:
- base_flat: bfloat16 [2, 29568, 8192], P(None, ('row', 'col')), may hold values from -6 to 6
- adjusted_flat: bfloat16 [2, 29568, 8192], P(None, ('row', 'col')), may hold values from -6 to 6
- omega: bfloat16 [2, 8192, 256], P(None, 'col'), may hold values from -6 to 6
Outputs:
- adapter_up_basis: float32 [2, 29568, 256], P(None, ('row', 'col'))
- adapter_down_transposed: float32 [2, 8192, 256], P(None, 'col', 'row')
The draws below stay inside these ranges and needn't reach their ends.
All inputs are finite; a program needn't handle non-finite values.
Results may differ from the reference program's by a relative error of at most 0.011.
Values may be sent and summed in bfloat16 or wider, within the bound.
A program may use at most 128 MiB of HBM per device.

```python
import math
import jax
import jax.numpy as jnp
from jax import lax

HIDDEN_UNITS = 29568
N = 8192
K = 256
MATS = 2


def levels(stream_key, dims, split, smallest, top_value):
    factor_of = 1.0
    for dim, parts in split:
        steps = jax.random.uniform(jax.random.fold_in(jax.random.fold_in(stream_key, 6), dim), (parts,), jnp.float32, smallest / len(split), top_value / len(split))
        factor_of = factor_of * jnp.repeat(jnp.exp(steps), dims[dim] // parts).reshape((-1,) + (1,) * (len(dims) - 1 - dim))
    return factor_of


def gaussian(key, dims, spread, reach, pieces=(), kind=jnp.bfloat16):
    values = jax.random.normal(key, dims, jnp.float32) * spread
    if len(pieces) > 0:
        values = levels(key, dims, pieces, -0.22, 0.18) * values
    return jnp.clip(values, min=-reach, max=reach).astype(kind)


def setup_inputs(seed: int = 0) -> dict:
    streams_of = jax.random.split(jax.random.key(seed), 4)
    return {
        "base_flat": gaussian(streams_of[0], (MATS, HIDDEN_UNITS, N), 1.0, 6.0, ((1, 128),)),
        "adjusted_flat": gaussian(streams_of[1], (MATS, HIDDEN_UNITS, N), 1.0, 6.0, ((1, 128),)),
        "omega": gaussian(streams_of[2], (MATS, N, K), 1.0, 6.0, ((1, 16),)),
    }


def product(left, right):
    return jnp.dot(left.astype(jnp.float32), right.astype(jnp.float32), precision=lax.Precision.HIGHEST)

def orthonormal(panel):
    gram = jnp.dot(panel.T, panel, precision=lax.Precision.HIGHEST)
    lower = jnp.linalg.cholesky(gram)
    solved = jax.scipy.linalg.solve_triangular(lower, panel.T, lower=True)
    return solved.T

def reference(base_flat, adjusted_flat, omega):
    ups = []
    downs = []
    for index in range(MATS):
        delta = (adjusted_flat[index].astype(jnp.float32) - base_flat[index].astype(jnp.float32)).astype(jnp.bfloat16)
        sketch = product(delta, omega[index])
        first_basis = orthonormal(sketch).astype(jnp.bfloat16)
        columns = product(delta.T, first_basis).astype(jnp.bfloat16)
        power = product(delta, columns)
        basis = orthonormal(power)
        ups.append(math.sqrt(HIDDEN_UNITS) * basis)
        downs.append(product(delta.T, basis.astype(jnp.bfloat16)))
    return (jnp.stack(ups), jnp.stack(downs))
```

```python
import math

import jax
import jax.numpy as jnp
from jax import lax
from jax.experimental import pallas as pl
from jax.experimental.pallas import tpu as pltpu
from jax.sharding import PartitionSpec as P

HI = lax.Precision.HIGHEST
MESH = pl.DeviceIdType.MESH
NB = 16
ROWS, PAD, WIDE, RANK, SUB = 231, 240, 512, 256, 128
ORDERS = ((0, 1, 2), (1, 2, 0), (2, 0, 1))
CUT_RS = ((0, 96), (96, 80), (176, 80))
CUT_AG = ((0, 48), (48, 48), (96, 32))


def dot(a, b, ca, cb, precision=None):
    return lax.dot_general(a, b, (((ca,), (cb,)), ((), ())), precision=precision, preferred_element_type=jnp.float32)

def factor_panel(work):
    size = 128
    lane = lax.broadcasted_iota(jnp.int32, (NB, size), 1)
    sub = lax.broadcasted_iota(jnp.int32, (NB, size), 0)
    def step(k, carry):
        start = pl.multiple_of(k * NB, NB)
        rows = work[pl.ds(start, NB), :]
        x = pltpu.roll(rows[:, :size], lax.rem(size - start, size), 1)
        x = jnp.where(lane < NB, x, jnp.where(lane == sub + NB, 1.0, 0.0))
        for j in range(NB - 1):
            inv = 1.0 / x[j : j + 1, j : j + 1]
            mult = x[:, j : j + 1] * inv
            mult = jnp.where(sub > j, jnp.broadcast_to(mult, (NB, size)), 0.0)
            x = x - mult * jnp.broadcast_to(x[j : j + 1, :], (NB, size))
        diag = jnp.sum(jnp.where(lane == sub, x, 0.0), axis=1, keepdims=True)
        t = x[:, NB : 2 * NB] * lax.rsqrt(diag)
        new = dot(t, rows, 1, 0, HI)
        left = jnp.where(lane >= start + NB, new[:, :size], 0.0)
        work[...] -= dot(left, new, 0, 0, HI)
        work[pl.ds(start, NB), :] = new
        return carry
    lax.fori_loop(0, size // NB, step, 0)

def invert_factor(gram, work, out):
    size = 128
    eye = (lax.broadcasted_iota(jnp.int32, (size, size), 0) == lax.broadcasted_iota(jnp.int32, (size, size), 1)).astype(jnp.float32)
    work[:, :size] = gram[0:16].reshape(size, size)
    work[:, size:] = eye
    factor_panel(work)
    t11 = work[:, size:]
    l21 = dot(gram[16:32].reshape(size, size), t11, 1, 1, HI)
    out[:size, :size] = t11
    out[:size, size:] = jnp.zeros((size, size), jnp.float32)
    out[size:, :size] = dot(l21, t11, 1, 0, HI)
    work[:, :size] = gram[48:64].reshape(size, size) - dot(l21, l21, 1, 1, HI)
    work[:, size:] = eye
    factor_panel(work)
    t22 = work[:, size:]
    out[size:, :size] = -dot(t22, out[size:, :size], 1, 0, HI)
    out[size:, size:] = t22


def device_at(pos, core):
    x, y, z = pos
    return {"row": lax.rem(y, 2) * 4 + z, "col": x * 4 + lax.div(y, 2) * 2 + core}


def moved(pos, axis, step):
    return tuple(lax.rem(p + step, 4) if a == axis else p for a, p in enumerate(pos))


def send(src, dst, send_sem, recv_sem, device):
    return pltpu.make_async_remote_copy(
        src_ref=src, dst_ref=dst, send_sem=send_sem, recv_sem=recv_sem, device_id=device, device_id_type=MESH
    )


def reduce_scatter(pos, core, source, bufs, total, send_sems, recv_sems):
    copies = {}

    def launch(part, stage, block):
        axis = ORDERS[part][stage]
        copies[part, stage] = []
        for step in (2, 1, 3):
            to = moved(pos, axis, step)
            copy = send(
                block(to[axis]),
                bufs[part][2 * stage].at[step - 1],
                send_sems.at[part, stage, step - 1],
                recv_sems.at[part, stage, step - 1],
                device_at(to, core),
            )
            copy.start()
            copies[part, stage].append(copy)

    def first(part, at):
        start, size = CUT_RS[part]
        rows = pl.ds(start, size)
        axis = ORDERS[part][0]
        if axis == 0:
            return source.at[at, :, :, rows]
        if axis == 1:
            return source.at[:, at, :, rows]
        return source.at[:, :, at, rows]

    def second(part, at):
        held = bufs[part][1]
        return held.at[:, at] if part == 1 else held.at[at]

    def arrived(part, stage):
        for copy in copies[part, stage]:
            copy.wait_recv()

    for part in range(3):
        launch(part, 0, lambda at, part=part: first(part, at))
    for part in range(3):
        arrived(part, 0)
        here, got, held = first(part, pos[ORDERS[part][0]]), bufs[part][0], bufs[part][1]

        @pl.loop(0, 16)
        def _(n, here=here, got=got, held=held):
            a, b = lax.div(n, 4), lax.rem(n, 4)
            value = here[a, b].astype(jnp.float32)
            for step in range(3):
                value += got[step, a, b].astype(jnp.float32)
            held[a, b] = value.astype(jnp.bfloat16)

        launch(part, 1, lambda at, part=part: second(part, at))
    for part in range(3):
        arrived(part, 1)
        here, got, held = second(part, pos[ORDERS[part][1]]), bufs[part][2], bufs[part][3]
        for a in range(4):
            value = here[a].astype(jnp.float32)
            for step in range(3):
                value += got[step, a].astype(jnp.float32)
            held[a] = value.astype(jnp.bfloat16)
        launch(part, 2, lambda at, held=held: held.at[at])
    for part in range(3):
        arrived(part, 2)
        start, size = CUT_RS[part]
        value = bufs[part][3][pos[ORDERS[part][2]]].astype(jnp.float32)
        for step in range(3):
            value += bufs[part][4][step].astype(jnp.float32)
        total[start : start + size, :] = value
    for part in range(3):
        for stage in range(3):
            for copy in copies[part, stage]:
                copy.wait_send()


def all_gather(pos, core, blocks, send_sems, recv_sems):
    copies = {}

    def launch(part, stage):
        start, size = CUT_AG[part]
        done = ORDERS[part][:stage]
        index = tuple(slice(None) if a in done else pos[a] for a in range(3)) + (pl.ds(start, size),)
        axis = ORDERS[part][stage]
        copies[part, stage] = []
        for step in (2, 1, 3):
            copy = send(
                blocks.at[index],
                blocks.at[index],
                send_sems.at[part, stage, step - 1],
                recv_sems.at[part, stage, step - 1],
                device_at(moved(pos, axis, step), core),
            )
            copy.start()
            copies[part, stage].append(copy)

    for stage in range(3):
        for part in range(3):
            if stage:
                for copy in copies[part, stage - 1]:
                    copy.wait_recv()
            launch(part, stage)
    for part in range(3):
        for copy in copies[part, 2]:
            copy.wait_recv()
    for part in range(3):
        for stage in range(3):
            for copy in copies[part, stage]:
                copy.wait_send()


def gram_sum(pos, core, panel, pieces, got, mine, whole, sems):
    chip = pos[0] * 16 + pos[1] * 4 + pos[2]
    gram = dot(panel, panel, 0, 0, HI)
    pieces[0:32] = gram[:, :SUB].reshape(32, 8, SUB)
    pieces[32:64] = gram[:, SUB:].reshape(32, 8, SUB)

    def peer(step):
        to = lax.rem(chip + step, 64)
        return to, device_at((lax.div(to, 16), lax.rem(lax.div(to, 4), 4), lax.rem(to, 4)), core)

    @pl.loop(1, 64)
    def _(step):
        to, device = peer(step)
        send(pieces.at[to], got.at[step], sems.at[0], sems.at[1], device).start()

    got[0] = pieces[chip]
    everyone = send(pieces.at[pl.ds(1, 63)], got.at[pl.ds(1, 63)], sems.at[0], sems.at[1], peer(1)[1])
    everyone.wait_recv()
    value = jnp.sum(got[...], axis=0)
    mine[...] = value
    whole[chip] = value

    @pl.loop(1, 64)
    def _(step):
        send(mine, whole.at[chip], sems.at[2], sems.at[3], peer(step)[1]).start()

    everyone.wait_send()
    last = send(got.at[pl.ds(1, 63)], whole.at[pl.ds(1, 63)], sems.at[2], sems.at[3], peer(1)[1])
    last.wait_recv()
    last.wait_send()


def kernel(base, adjusted, omega, up, down, *scratch):
    (
        load_base, load_adjusted, load_sems, delta, outgoing, delta_sems, sketch_map, map_sems,
        sketch, sketch_got, power, power_got, swap_sems, turned, source,
        *rest,
    ) = scratch
    bufs = [rest[5 * part : 5 * part + 5] for part in range(3)]
    (
        total, rs_send, rs_recv, columns, ag_send, ag_recv,
        pieces, gram_got, gram_mine, gram, gram_sems, work, factor, spread, spread_send, spread_recv,
    ) = rest[15:]
    row, col = lax.axis_index("row"), lax.axis_index("col")
    core = lax.rem(col, 2)
    pos = (lax.div(col, 4), lax.rem(lax.div(col, 2), 2) * 2 + lax.div(row, 4), lax.rem(row, 4))
    mate = device_at(pos, 1 - core)
    own = lax.div(col, 2)
    chip = pos[0] * 16 + pos[1] * 4 + pos[2]

    def load(n):
        slot = n % 4
        block = 2 * (n % 8) + ((1 - core) if n < 8 else core)
        lanes = pl.ds(pl.multiple_of(block * WIDE, WIDE), WIDE)
        return (
            pltpu.make_async_copy(base.at[:, :, lanes], load_base.at[slot], load_sems.at[slot, 0]),
            pltpu.make_async_copy(adjusted.at[:, :, lanes], load_adjusted.at[slot], load_sems.at[slot, 1]),
        )

    for n in range(4):
        for copy in load(n):
            copy.start()
    own_map = pltpu.make_async_copy(omega, sketch_map.at[own], map_sems.at[14])
    own_map.start()

    barrier = pltpu.get_barrier_semaphore()
    pl.semaphore_signal(barrier, 1, device_id=mate, device_id_type=MESH)

    @pl.loop(1, 64)
    def _(step):
        to = lax.rem(chip + step, 64)
        device = device_at((lax.div(to, 16), lax.rem(lax.div(to, 4), 4), lax.rem(to, 4)), core)
        pl.semaphore_signal(barrier, 1, device_id=device, device_id_type=MESH)

    pl.semaphore_wait(barrier, 64)

    map_copies = []
    for step in range(1, 8):
        far = (lax.rem(pos[0] + step // 2, 4), lax.rem(pos[1] + 2 * (step % 2), 4), pos[2])
        copy = send(omega, sketch_map.at[own], map_sems.at[step - 1], map_sems.at[step + 6], device_at(far, core))
        copy.start()
        map_copies.append(copy)

    delta_copies = []
    zeros = jnp.zeros((2, PAD - 224, WIDE), jnp.bfloat16)
    for n in range(16):
        for copy in load(n):
            copy.wait()
        place = outgoing.at[n] if n < 8 else delta.at[n - 8, core]
        place[:, 224:, :] = zeros
        for m in range(2):
            value = load_adjusted[n % 4, m].astype(jnp.float32) - load_base[n % 4, m].astype(jnp.float32)
            place[m, 0:ROWS, :] = value.astype(jnp.bfloat16)
        if n < 12:
            for copy in load(n + 4):
                copy.start()
        if n < 8:
            copy = send(outgoing.at[n], delta.at[n, core], delta_sems.at[0, n], delta_sems.at[1, n], mate)
            copy.start()
            delta_copies.append(copy)
    own_map.wait()
    for copy in map_copies + delta_copies:
        copy.wait()

    def swap(part, got, which):
        copy = send(part, got, swap_sems.at[0, which], swap_sems.at[1, which], mate)
        copy.start()
        copy.wait()

    def product(right, part):
        for m in range(2):
            part[m] = jnp.zeros((2 * PAD, RANK), jnp.float32)

            @pl.loop(0, 8)
            def _(i, m=m):
                part[m] += dot(delta[i, :, m].reshape(2 * PAD, WIDE), right(i, m), 1, 0)

    def folded():
        for m in range(2):

            @pl.loop(0, 8)
            def _(i, m=m):
                value = dot(turned[m], delta[i, :, m].reshape(2 * PAD, WIDE), 1, 0).astype(jnp.bfloat16)
                for z in range(4):
                    source[lax.div(i, 2), lax.rem(i, 2) * 2 + m, z] = value[:, z * SUB : (z + 1) * SUB]

        reduce_scatter(pos, core, source, bufs, total, rs_send, rs_recv)

    def orthonormal(panel, which):
        gram_sum(pos, core, panel[core], pieces, gram_got, gram_mine, gram, gram_sems)
        invert_factor(gram, work, factor.at[core])
        swap(factor.at[core], factor.at[core], which)
        for m in range(2):
            turned[m] = dot(factor[m], panel[m], 1, 1, HI).astype(jnp.bfloat16)

    product(lambda i, m: sketch_map[i, m], sketch)
    swap(sketch, sketch_got, 0)
    sketch[...] += sketch_got[...]
    orthonormal(sketch, 1)
    folded()
    columns[pos[0], pos[1], pos[2]] = total[...].T.astype(jnp.bfloat16)
    all_gather(pos, core, columns, ag_send, ag_recv)
    product(
        lambda i, m: columns[lax.div(i, 2), lax.rem(i, 2) * 2 + m].reshape(WIDE, RANK),
        power,
    )
    swap(power, power_got, 2)
    power[...] += power_got[...]
    orthonormal(power, 3)
    for m in range(2):
        rows = power[m, pl.ds(pl.multiple_of(core * PAD, PAD), PAD), :]
        up[m] = (dot(rows, factor[m], 1, 1, HI) * math.sqrt(29568))[:ROWS]
    folded()

    spread_copies = []
    for step in range(1, 8):
        to = lax.rem(row + step, 8)
        rows = pl.ds(pl.multiple_of(to * 32, 32), 32)
        copy = send(
            total.at[rows],
            spread.at[row],
            spread_send.at[step - 1],
            spread_recv.at[step - 1],
            {"row": to, "col": col},
        )
        copy.start()
        spread_copies.append(copy)
    spread[row] = total[pl.ds(pl.multiple_of(row * 32, 32), 32), :]
    for copy in spread_copies:
        copy.wait()
    for n in range(8):
        down[n // 4, (n % 4) * SUB : (n % 4 + 1) * SUB, :] = spread[n].T


def scratch_shapes():
    half, full = jnp.bfloat16, jnp.float32
    dma = pltpu.SemaphoreType.DMA
    parts = []
    for _, size in CUT_RS:
        parts += [
            pltpu.VMEM((3, 4, 4, size, SUB), half),
            pltpu.VMEM((4, 4, size, SUB), half),
            pltpu.VMEM((3, 4, size, SUB), half),
            pltpu.VMEM((4, size, SUB), half),
            pltpu.VMEM((3, size, SUB), half),
        ]
    return [
        pltpu.VMEM((4, 2, ROWS, WIDE), half),
        pltpu.VMEM((4, 2, ROWS, WIDE), half),
        dma((4, 2)),
        pltpu.VMEM((8, 2, 2, PAD, WIDE), half),
        pltpu.VMEM((8, 2, PAD, WIDE), half),
        dma((2, 8)),
        pltpu.VMEM((8, 2, WIDE, RANK), half),
        dma((15,)),
        pltpu.VMEM((2, 2 * PAD, RANK), full),
        pltpu.VMEM((2, 2 * PAD, RANK), full),
        pltpu.VMEM((2, 2 * PAD, RANK), full),
        pltpu.VMEM((2, 2 * PAD, RANK), full),
        dma((2, 4)),
        pltpu.VMEM((2, RANK, 2 * PAD), half),
        pltpu.VMEM((4, 4, 4, RANK, SUB), half),
        *parts,
        pltpu.VMEM((RANK, SUB), full),
        dma((3, 3, 3)),
        dma((3, 3, 3)),
        pltpu.VMEM((4, 4, 4, SUB, RANK), half),
        dma((3, 3, 3)),
        dma((3, 3, 3)),
        pltpu.VMEM((64, 8, SUB), full),
        pltpu.VMEM((64, 8, SUB), full),
        pltpu.VMEM((8, SUB), full),
        pltpu.VMEM((64, 8, SUB), full),
        dma((4,)),
        pltpu.VMEM((SUB, 2 * SUB), full),
        pltpu.VMEM((2, RANK, RANK), full),
        pltpu.VMEM((8, 32, SUB), full),
        dma((7,)),
        dma((7,)),
    ]


def local(base_flat, adjusted_flat, omega):
    anywhere = pl.BlockSpec(memory_space=pl.ANY)
    vmem = pl.BlockSpec(memory_space=pltpu.VMEM)
    return pl.pallas_call(
        kernel,
        out_shape=(
            jax.ShapeDtypeStruct((2, ROWS, RANK), jnp.float32),
            jax.ShapeDtypeStruct((2, WIDE, 32), jnp.float32),
        ),
        in_specs=[anywhere] * 3,
        out_specs=(vmem, vmem),
        scratch_shapes=scratch_shapes(),
        compiler_params=pltpu.CompilerParams(
            collective_id=0, has_side_effects=True, vmem_limit_bytes=60 * 2**20
        ),
    )(base_flat, adjusted_flat, omega)


def solution(mesh):
    in_specs = (P(None, ("row", "col"), None), P(None, ("row", "col"), None), P(None, "col", None))
    out_specs = (P(None, ("row", "col"), None), P(None, "col", "row"))
    return jax.shard_map(local, mesh=mesh, in_specs=in_specs, out_specs=out_specs, check_vma=False)
```

```python
import math

import jax
import jax.numpy as jnp
from jax import lax
from jax.experimental import pallas as pl
from jax.experimental.pallas import tpu as pltpu
from jax.sharding import PartitionSpec as P

HI = lax.Precision.HIGHEST
MESH = pl.DeviceIdType.MESH
NB = 16
ROWS, PAD, WIDE, RANK, SUB = 231, 240, 512, 256, 128
ORDERS = ((0, 1, 2), (1, 2, 0), (2, 0, 1))
CUT_RS = ((0, 96), (96, 80), (176, 80))
CUT_AG = ((0, 48), (48, 48), (96, 32))
ORDERS_MAP = ((1, 0, 2), (1, 2, 0), (0, 2, 1))


def dot(a, b, ca, cb, precision=None):
    return lax.dot_general(a, b, (((ca,), (cb,)), ((), ())), precision=precision, preferred_element_type=jnp.float32)

def factor_panel(work):
    size = 128
    lane = lax.broadcasted_iota(jnp.int32, (NB, size), 1)
    sub = lax.broadcasted_iota(jnp.int32, (NB, size), 0)

    def wide(row):
        return jnp.broadcast_to(row, (NB, size))

    def step(k, carry):
        start = pl.multiple_of(k * NB, NB)
        left, right = work[pl.ds(start, NB), :size], work[pl.ds(start, NB), size:]
        block = pltpu.roll(left, lax.rem(size - start, size), 1)
        cols = [wide(block[:, j : j + 1]) for j in range(NB)]
        diag = cols[0]
        for j in range(NB - 1):
            mult = jnp.where(sub > j, cols[j] * wide(1.0 / cols[j][j : j + 1, :]), 0.0)
            for n in range(j + 1, NB):
                cols[n] = cols[n] - mult * wide(cols[n][j : j + 1, :])
            left = left - mult * wide(left[j : j + 1, :])
            right = right - mult * wide(right[j : j + 1, :])
            diag = jnp.where(sub > j, cols[j + 1], diag)
        scale = lax.rsqrt(diag)
        left, right = left * scale, right * scale
        below = jnp.where(lane >= start + NB, left, 0.0)
        new = jnp.concatenate([left, right], axis=1)
        work[...] -= dot(below, new, 0, 0, HI)
        work[pl.ds(start, NB), :] = new
        return carry
    lax.fori_loop(0, size // NB, step, 0)

def invert_factor(gram, work, out):
    size = 128
    eye = (lax.broadcasted_iota(jnp.int32, (size, size), 0) == lax.broadcasted_iota(jnp.int32, (size, size), 1)).astype(jnp.float32)
    work[:, :size] = gram[0:16].reshape(size, size)
    work[:, size:] = eye
    factor_panel(work)
    t11 = work[:, size:]
    l21 = dot(gram[16:32].reshape(size, size), t11, 1, 1, HI)
    out[:size, :size] = t11
    out[:size, size:] = jnp.zeros((size, size), jnp.float32)
    out[size:, :size] = dot(l21, t11, 1, 0, HI)
    work[:, :size] = gram[48:64].reshape(size, size) - dot(l21, l21, 1, 1, HI)
    work[:, size:] = eye
    factor_panel(work)
    t22 = work[:, size:]
    out[size:, :size] = -dot(t22, out[size:, :size], 1, 0, HI)
    out[size:, size:] = t22


def device_at(pos, core):
    x, y, z = pos
    return {"row": lax.rem(y, 2) * 4 + z, "col": x * 4 + lax.div(y, 2) * 2 + core}


def moved(pos, axis, step):
    return tuple(lax.rem(p + step, 4) if a == axis else p for a, p in enumerate(pos))


def send(src, dst, send_sem, recv_sem, device):
    return pltpu.make_async_remote_copy(
        src_ref=src, dst_ref=dst, send_sem=send_sem, recv_sem=recv_sem, device_id=device, device_id_type=MESH
    )


def reduce_scatter(pos, core, source, fill, bufs, total, send_sems, recv_sems, slab_sems):
    copies = {}

    def launch(part, stage, block):
        axis = ORDERS[part][stage]
        copies[part, stage] = []
        for step in (2, 1, 3):
            to = moved(pos, axis, step)
            copy = send(
                block(to[axis]),
                bufs[part][2 * stage].at[step - 1],
                send_sems.at[part, stage, step - 1],
                recv_sems.at[part, stage, step - 1],
                device_at(to, core),
            )
            copy.start()
            copies[part, stage].append(copy)

    def first(part, at):
        start, size = CUT_RS[part]
        rows = pl.ds(start, size)
        axis = ORDERS[part][0]
        if axis == 0:
            return source.at[at, :, :, rows]
        if axis == 1:
            return source.at[:, at, :, rows]
        return source.at[:, :, at, rows]

    def second(part, at):
        held = bufs[part][1]
        return held.at[:, at] if part == 1 else held.at[at]

    def arrived(part, stage):
        for copy in copies[part, stage]:
            copy.wait_recv()

    for part in range(3):
        copies[part, 0] = []
    for slab in (2, 1, 3, 0):
        x = lax.rem(pos[0] + slab, 4)
        fill(x)
        if slab:
            copy = send(
                first(0, x),
                bufs[0][0].at[slab - 1],
                send_sems.at[0, 0, slab - 1],
                recv_sems.at[0, 0, slab - 1],
                device_at(moved(pos, 0, slab), core),
            )
            copy.start()
            copies[0, 0].append(copy)
        for part in (1, 2):
            start, size = CUT_RS[part]
            rows = pl.ds(start, size)
            for step in (2, 1, 3):
                to = moved(pos, part, step)
                block = source.at[x, to[1], :, rows] if part == 1 else source.at[x, :, to[2], rows]
                copy = send(
                    block,
                    bufs[part][0].at[step - 1, x],
                    slab_sems.at[0, part - 1, slab, step - 1],
                    slab_sems.at[1, part - 1, x, step - 1],
                    device_at(to, core),
                )
                copy.start()
                copies[part, 0].append(copy)
    for part in range(3):
        arrived(part, 0)
        here, got, held = first(part, pos[ORDERS[part][0]]), bufs[part][0], bufs[part][1]

        @pl.loop(0, 16)
        def _(n, here=here, got=got, held=held):
            a, b = lax.div(n, 4), lax.rem(n, 4)
            value = here[a, b].astype(jnp.float32)
            for step in range(3):
                value += got[step, a, b].astype(jnp.float32)
            held[a, b] = value.astype(jnp.bfloat16)

        launch(part, 1, lambda at, part=part: second(part, at))
    for part in range(3):
        arrived(part, 1)
        here, got, held = second(part, pos[ORDERS[part][1]]), bufs[part][2], bufs[part][3]
        for a in range(4):
            value = here[a].astype(jnp.float32)
            for step in range(3):
                value += got[step, a].astype(jnp.float32)
            held[a] = value.astype(jnp.bfloat16)
        launch(part, 2, lambda at, held=held: held.at[at])
    for part in range(3):
        arrived(part, 2)
        start, size = CUT_RS[part]
        value = bufs[part][3][pos[ORDERS[part][2]]].astype(jnp.float32)
        for step in range(3):
            value += bufs[part][4][step].astype(jnp.float32)
        total[start : start + size, :] = value
    for part in range(3):
        for stage in range(3):
            for copy in copies[part, stage]:
                copy.wait_send()


def all_gather(pos, core, blocks, send_sems, recv_sems):
    copies = {}

    def launch(part, stage):
        start, size = CUT_AG[part]
        done = ORDERS[part][:stage]
        index = tuple(slice(None) if a in done else pos[a] for a in range(3)) + (pl.ds(start, size),)
        axis = ORDERS[part][stage]
        copies[part, stage] = []
        for step in (2, 1, 3):
            copy = send(
                blocks.at[index],
                blocks.at[index],
                send_sems.at[part, stage, step - 1],
                recv_sems.at[part, stage, step - 1],
                device_at(moved(pos, axis, step), core),
            )
            copy.start()
            copies[part, stage].append(copy)

    for stage in range(3):
        for part in range(3):
            if stage:
                for copy in copies[part, stage - 1]:
                    copy.wait_recv()
            launch(part, stage)
    for part in range(3):
        for copy in copies[part, 2]:
            copy.wait_recv()
    for part in range(3):
        for stage in range(3):
            for copy in copies[part, stage]:
                copy.wait_send()


def gram_sum(pos, core, panel, pieces, got, mine, whole, sems):
    chip = pos[0] * 16 + pos[1] * 4 + pos[2]
    gram = dot(panel, panel, 0, 0, HI)
    pieces[0:32] = gram[:, :SUB].reshape(32, 8, SUB)
    pieces[32:64] = gram[:, SUB:].reshape(32, 8, SUB)

    def peer(step):
        to = lax.rem(chip + step, 64)
        return to, device_at((lax.div(to, 16), lax.rem(lax.div(to, 4), 4), lax.rem(to, 4)), core)

    @pl.loop(1, 64)
    def _(step):
        to, device = peer(step)
        send(pieces.at[to], got.at[step], sems.at[0], sems.at[1], device).start()

    got[0] = pieces[chip]
    everyone = send(pieces.at[pl.ds(1, 63)], got.at[pl.ds(1, 63)], sems.at[0], sems.at[1], peer(1)[1])
    everyone.wait_recv()
    value = jnp.sum(got[...], axis=0)
    mine[...] = value
    whole[chip] = value

    @pl.loop(1, 64)
    def _(step):
        send(mine, whole.at[chip], sems.at[2], sems.at[3], peer(step)[1]).start()

    everyone.wait_send()
    last = send(got.at[pl.ds(1, 63)], whole.at[pl.ds(1, 63)], sems.at[2], sems.at[3], peer(1)[1])
    last.wait_recv()
    last.wait_send()


def kernel(base, adjusted, omega, up, down, *scratch):
    (
        load_base, load_adjusted, load_sems, apart, delta, outgoing, delta_sems, sketch_map, map_sems,
        sketch, sketch_got, power, power_got, swap_sems, turned, source,
        *rest,
    ) = scratch
    bufs = [rest[5 * part : 5 * part + 5] for part in range(3)]
    (
        total, rs_send, rs_recv, slab_sems, columns, ag_send, ag_recv,
        pieces, gram_got, gram_mine, gram, gram_sems, work, factor, spread, spread_send, spread_recv,
    ) = rest[15:]
    row, col = lax.axis_index("row"), lax.axis_index("col")
    core = lax.rem(col, 2)
    pos = (lax.div(col, 4), lax.rem(lax.div(col, 2), 2) * 2 + lax.div(row, 4), lax.rem(row, 4))
    mate = device_at(pos, 1 - core)

    yh = lax.div(pos[1], 2)
    spot = (pos[0], yh, pos[2])

    def load(n):
        slot = lax.rem(n, 4)
        block = 2 * lax.rem(n, 8) + jnp.where(n < 8, 1 - core, core)
        copies = []
        for tile in range(4):
            lanes = pl.ds(pl.multiple_of(block * WIDE + tile * SUB, SUB), SUB)
            for which, (array, held) in enumerate(((base, load_base), (adjusted, load_adjusted))):
                copies.append(
                    pltpu.make_async_copy(array.at[:, :, lanes], held.at[slot, tile], load_sems.at[slot, which, tile])
                )
        return copies

    for n in range(4):
        for copy in load(n):
            copy.start()
    quarter = pl.ds(pl.multiple_of(pos[2] * SUB, SUB), SUB)
    own_map = pltpu.make_async_copy(omega.at[:, quarter], sketch_map.at[spot], map_sems.at[0, 0, 0, 0])
    own_map.start()

    barrier = pltpu.get_barrier_semaphore()
    near = [moved(pos, axis, step) for axis in (0, 2) for step in (1, 2, 3)]
    near += [(pos[0], 3 - pos[1], pos[2]), (pos[0], pos[1] + 1 - 2 * lax.rem(pos[1], 2), pos[2])]
    for device in [mate] + [device_at(to, core) for to in near]:
        pl.semaphore_signal(barrier, 1, device_id=device, device_id_type=MESH)
    pl.semaphore_wait(barrier, 9)

    map_copies = {}

    def launch_map(stage):
        for part in range(3):
            start, size = CUT_AG[part]
            order = ORDERS_MAP[part]
            if stage:
                for copy in map_copies[part, stage - 1]:
                    copy.wait_recv()
            index = tuple(slice(None) if a in order[:stage] else spot[a] for a in range(3))
            block = sketch_map.at[index + (slice(None), pl.ds(start, size))]
            axis = order[stage]
            map_copies[part, stage] = []
            for step in (2, 1, 3) if axis != 1 else (1,):
                to = (pos[0], 3 - pos[1], pos[2]) if axis == 1 else moved(pos, axis, step)
                copy = send(
                    block,
                    block,
                    map_sems.at[1, part, stage, step - 1],
                    map_sems.at[2, part, stage, step - 1],
                    device_at(to, core),
                )
                copy.start()
                map_copies[part, stage].append(copy)

    own_map.wait()
    launch_map(0)
    zeros = jnp.zeros((2, PAD - 224, WIDE), jnp.bfloat16)

    def subtract(low, high, leaving):
        @pl.loop(low, high)
        def _(n):
            slot = lax.rem(n, 4)
            for copy in load(n):
                copy.wait()
            place = outgoing.at[n] if leaving else delta.at[n - 8, core]
            place[:, 224:, :] = zeros
            for tile in range(4):
                value = load_adjusted[slot, tile].astype(jnp.float32) - load_base[slot, tile].astype(jnp.float32)
                apart[tile, 0 : 2 * ROWS] = value.reshape(2 * ROWS, SUB)
                for m in range(2):
                    rows = apart[tile, pl.ds(m, ROWS, stride=2), :]
                    place[m, 0:ROWS, tile * SUB : (tile + 1) * SUB] = rows.astype(jnp.bfloat16)

            @pl.when(n < 12)
            def _():
                for copy in load(n + 4):
                    copy.start()

            if leaving:
                send(outgoing.at[n], delta.at[n, core], delta_sems.at[0, n], delta_sems.at[1, n], mate).start()

    subtract(0, 3, True)
    launch_map(1)
    subtract(3, 8, True)
    subtract(8, 9, False)
    launch_map(2)
    subtract(9, 16, False)
    for n in range(8):
        send(outgoing.at[n], delta.at[n, core], delta_sems.at[0, n], delta_sems.at[1, n], mate).wait()
    for part in range(3):
        for copy in map_copies[part, 2]:
            copy.wait_recv()
    for copies in map_copies.values():
        for copy in copies:
            copy.wait_send()

    def swap(part, got, which):
        copy = send(part, got, swap_sems.at[0, which], swap_sems.at[1, which], mate)
        copy.start()
        copy.wait()

    def product(right, part):
        for m in range(2):
            part[m] = jnp.zeros((2 * PAD, RANK), jnp.float32)

            @pl.loop(0, 8)
            def _(i, m=m):
                part[m] += dot(delta[i, :, m].reshape(2 * PAD, WIDE), right(i, m), 1, 0)

    def folded():
        def fill(x):
            @pl.loop(0, 2)
            def _(n):
                for m in range(2):
                    value = dot(turned[m], delta[x * 2 + n, :, m].reshape(2 * PAD, WIDE), 1, 0).astype(jnp.bfloat16)
                    for z in range(4):
                        source[x, n * 2 + m, z] = value[:, z * SUB : (z + 1) * SUB]

        reduce_scatter(pos, core, source, fill, bufs, total, rs_send, rs_recv, slab_sems)

    def orthonormal(panel, which):
        gram_sum(pos, core, panel[core], pieces, gram_got, gram_mine, gram, gram_sems)
        invert_factor(gram, work, factor.at[core])
        swap(factor.at[core], factor.at[core], which)
        for m in range(2):
            turned[m] = dot(factor[m], panel[m], 1, 1, HI).astype(jnp.bfloat16)

    product(lambda i, m: sketch_map[lax.div(i, 2), lax.rem(i, 2), :, m].reshape(WIDE, RANK), sketch)
    swap(sketch, sketch_got, 0)
    sketch[...] += sketch_got[...]
    orthonormal(sketch, 1)
    folded()
    columns[pos[0], pos[1], pos[2]] = total[...].T.astype(jnp.bfloat16)
    all_gather(pos, core, columns, ag_send, ag_recv)
    product(
        lambda i, m: columns[lax.div(i, 2), lax.rem(i, 2) * 2 + m].reshape(WIDE, RANK),
        power,
    )
    swap(power, power_got, 2)
    power[...] += power_got[...]
    orthonormal(power, 3)
    for m in range(2):
        rows = power[m, pl.ds(pl.multiple_of(core * PAD, PAD), PAD), :]
        up[:, m, :] = (dot(rows, factor[m], 1, 1, HI) * math.sqrt(29568))[:ROWS]
    folded()

    spread_copies = []
    for step in range(1, 8):
        to = lax.rem(row + step, 8)
        rows = pl.ds(pl.multiple_of(to * 32, 32), 32)
        copy = send(
            total.at[rows],
            spread.at[row],
            spread_send.at[step - 1],
            spread_recv.at[step - 1],
            {"row": to, "col": col},
        )
        copy.start()
        spread_copies.append(copy)
    spread[row] = total[pl.ds(pl.multiple_of(row * 32, 32), 32), :]
    for copy in spread_copies:
        copy.wait()
    for n in range(8):
        down[n // 4, :, (n % 4) * SUB : (n % 4 + 1) * SUB] = spread[n]


def scratch_shapes():
    half, full = jnp.bfloat16, jnp.float32
    dma = pltpu.SemaphoreType.DMA
    parts = []
    for _, size in CUT_RS:
        parts += [
            pltpu.VMEM((3, 4, 4, size, SUB), half),
            pltpu.VMEM((4, 4, size, SUB), half),
            pltpu.VMEM((3, 4, size, SUB), half),
            pltpu.VMEM((4, size, SUB), half),
            pltpu.VMEM((3, size, SUB), half),
        ]
    return [
        pltpu.VMEM((4, 4, ROWS, 2, SUB), half),
        pltpu.VMEM((4, 4, ROWS, 2, SUB), half),
        dma((4, 2, 4)),
        pltpu.VMEM((4, 2 * PAD, SUB), full),
        pltpu.VMEM((8, 2, 2, PAD, WIDE), half),
        pltpu.VMEM((8, 2, PAD, WIDE), half),
        dma((2, 8)),
        pltpu.VMEM((4, 2, 4, 2, SUB, RANK), half),
        dma((3, 3, 3, 3)),
        pltpu.VMEM((2, 2 * PAD, RANK), full),
        pltpu.VMEM((2, 2 * PAD, RANK), full),
        pltpu.VMEM((2, 2 * PAD, RANK), full),
        pltpu.VMEM((2, 2 * PAD, RANK), full),
        dma((2, 4)),
        pltpu.VMEM((2, RANK, 2 * PAD), half),
        pltpu.VMEM((4, 4, 4, RANK, SUB), half),
        *parts,
        pltpu.VMEM((RANK, SUB), full),
        dma((3, 3, 3)),
        dma((3, 3, 3)),
        dma((2, 2, 4, 3)),
        pltpu.VMEM((4, 4, 4, SUB, RANK), half),
        dma((3, 3, 3)),
        dma((3, 3, 3)),
        pltpu.VMEM((64, 8, SUB), full),
        pltpu.VMEM((64, 8, SUB), full),
        pltpu.VMEM((8, SUB), full),
        pltpu.VMEM((64, 8, SUB), full),
        dma((4,)),
        pltpu.VMEM((SUB, 2 * SUB), full),
        pltpu.VMEM((2, RANK, RANK), full),
        pltpu.VMEM((8, 32, SUB), full),
        dma((7,)),
        dma((7,)),
    ]


def local(base_flat, adjusted_flat, omega):
    anywhere = pl.BlockSpec(memory_space=pl.ANY)
    vmem = pl.BlockSpec(memory_space=pltpu.VMEM)
    up, down = pl.pallas_call(
        kernel,
        out_shape=(
            jax.ShapeDtypeStruct((ROWS, 2, RANK), jnp.float32),
            jax.ShapeDtypeStruct((2, 32, WIDE), jnp.float32),
        ),
        in_specs=[anywhere] * 3,
        out_specs=(vmem, vmem),
        scratch_shapes=scratch_shapes(),
        compiler_params=pltpu.CompilerParams(
            collective_id=0, has_side_effects=True, vmem_limit_bytes=60 * 2**20
        ),
    )(base_flat.transpose(1, 0, 2), adjusted_flat.transpose(1, 0, 2), omega)
    return up.transpose(1, 0, 2), down.transpose(0, 2, 1)


def solution(mesh):
    in_specs = (P(None, ("row", "col"), None), P(None, ("row", "col"), None), P(None, "col", None))
    out_specs = (P(None, ("row", "col"), None), P(None, "col", "row"))
    return jax.shard_map(local, mesh=mesh, in_specs=in_specs, out_specs=out_specs, check_vma=False)
```

```python
import math

import jax
import jax.numpy as jnp
from jax import lax
from jax.experimental import pallas as pl
from jax.experimental.pallas import tpu as pltpu
from jax.sharding import PartitionSpec as P

HI = lax.Precision.HIGHEST
MESH = pl.DeviceIdType.MESH
NB = 16
ROWS, PAD, WIDE, RANK, SUB = 231, 240, 512, 256, 128
ORDERS = ((0, 1, 2), (1, 2, 0), (2, 0, 1)) * 2
CUT_RS = ((0, 48), (48, 32), (80, 48), (128, 48), (176, 48), (224, 32))
CUT_AG = ((0, 16), (16, 16), (32, 16), (48, 32), (80, 32), (112, 16))
PARTS = range(6)


def dot(a, b, ca, cb, precision=None):
    return lax.dot_general(a, b, (((ca,), (cb,)), ((), ())), precision=precision, preferred_element_type=jnp.float32)

def terms(value):
    high = value.astype(jnp.bfloat16)
    rest = value - high.astype(jnp.float32)
    middle = rest.astype(jnp.bfloat16)
    return high, middle, (rest - middle.astype(jnp.float32)).astype(jnp.bfloat16)


def factor_panel(work):
    size = 128
    sub = lax.broadcasted_iota(jnp.int32, (NB, size), 0)

    def wide(row):
        return jnp.broadcast_to(row, (NB, size))

    def step(k, carry):
        start = pl.multiple_of(k * NB, NB)
        left, right = work[pl.ds(start, NB), :size], work[pl.ds(start, NB), size:]
        block = pltpu.roll(left, lax.rem(size - start, size), 1)
        cols = [wide(block[:, j : j + 1]) for j in range(NB)]
        diag = cols[0]
        for j in range(NB - 1):
            mult = jnp.where(sub > j, cols[j] * wide(1.0 / cols[j][j : j + 1, :]), 0.0)
            for n in range(j + 1, NB):
                cols[n] = cols[n] - mult * wide(cols[n][j : j + 1, :])
            left = left - mult * wide(left[j : j + 1, :])
            right = right - mult * wide(right[j : j + 1, :])
            diag = jnp.where(sub > j, cols[j + 1], diag)
        scale = lax.rsqrt(diag)
        left, right = left * scale, right * scale
        new = jnp.concatenate([left, right], axis=1)
        high, middle, low = terms(new)
        ahead = jnp.where(lax.broadcasted_iota(jnp.int32, (6 * NB, size), 1) >= start + NB, 1.0, 0.0).astype(jnp.bfloat16)
        below = jnp.concatenate([t[:, :size] for t in (high, high, middle, high, low, middle)], axis=0) * ahead
        other = jnp.concatenate([high, middle, high, low, high, middle], axis=0)
        work[...] -= dot(below, other, 0, 0)
        work[pl.ds(start, NB), :] = new
        return carry
    lax.fori_loop(0, size // NB, step, 0)

def invert_factor(gram, work, out):
    size = 128
    eye = (lax.broadcasted_iota(jnp.int32, (size, size), 0) == lax.broadcasted_iota(jnp.int32, (size, size), 1)).astype(jnp.float32)
    work[:, :size] = gram[0:16].reshape(size, size)
    work[:, size:] = eye
    factor_panel(work)
    t11 = work[:, size:]
    l21 = dot(gram[16:32].reshape(size, size), t11, 1, 1, HI)
    out[:size, :size] = t11
    out[:size, size:] = jnp.zeros((size, size), jnp.float32)
    out[size:, :size] = dot(l21, t11, 1, 0, HI)
    work[:, :size] = gram[48:64].reshape(size, size) - dot(l21, l21, 1, 1, HI)
    work[:, size:] = eye
    factor_panel(work)
    t22 = work[:, size:]
    out[size:, :size] = -dot(t22, out[size:, :size], 1, 0, HI)
    out[size:, size:] = t22


def device_at(pos, core):
    x, y, z = pos
    return {"row": lax.rem(y, 2) * 4 + z, "col": x * 4 + lax.div(y, 2) * 2 + core}


def moved(pos, axis, step):
    return tuple(lax.rem(p + step, 4) if a == axis else p for a, p in enumerate(pos))


def send(src, dst, send_sem, recv_sem, device):
    return pltpu.make_async_remote_copy(
        src_ref=src, dst_ref=dst, send_sem=send_sem, recv_sem=recv_sem, device_id=device, device_id_type=MESH
    )


def reduce_scatter(pos, core, source, fill, bufs, total, send_sems, recv_sems, slab_sems, between):
    copies = {(part, 0): [] for part in PARTS}

    def begin(part, stage, src, dst, sem, step):
        copy = send(src, dst, *sem, device_at(moved(pos, ORDERS[part][stage], step), core))
        copy.start()
        copies[part, stage].append(copy)

    def launch(part, stage, block):
        axis = ORDERS[part][stage]
        copies[part, stage] = []
        for step in (2, 1, 3):
            sem = (send_sems.at[part, stage, step - 1], recv_sems.at[part, stage, step - 1])
            begin(part, stage, block(moved(pos, axis, step)[axis]), bufs[part][2 * stage].at[step - 1], sem, step)

    def slab_out(part, slab, x):
        rows = pl.ds(*CUT_RS[part])
        axis = ORDERS[part][0]
        if axis == 0:
            if slab:
                sem = (send_sems.at[part, 0, slab - 1], recv_sems.at[part, 0, slab - 1])
                begin(part, 0, source.at[x, :, :, rows], bufs[part][0].at[slab - 1], sem, slab)
            return
        for step in (2, 1, 3):
            to = moved(pos, axis, step)
            block = source.at[x, to[1], :, rows] if axis == 1 else source.at[x, :, to[2], rows]
            sem = (slab_sems.at[0, part, slab, step - 1], slab_sems.at[1, part, x, step - 1])
            begin(part, 0, block, bufs[part][0].at[step - 1, x], sem, step)

    def own(part):
        rows = pl.ds(*CUT_RS[part])
        return (
            lambda a, b: source.at[pos[0], a, b, rows],
            lambda a, b: source.at[a, pos[1], b, rows],
            lambda a, b: source.at[a, b, pos[2], rows],
        )[ORDERS[part][0]]

    def second(part, at):
        held = bufs[part][1]
        return held.at[:, at] if ORDERS[part][0] == 1 else held.at[at]

    def arrived(part, stage):
        for copy in copies[part, stage]:
            copy.wait_recv()

    slabs = [(slab, lax.rem(pos[0] + slab, 4)) for slab in (2, 1, 3, 0)]
    for slab, x in slabs:
        fill(x)
        for part in range(3):
            slab_out(part, slab, x)
    for slab, x in slabs:
        for part in range(3, 6):
            slab_out(part, slab, x)
    between()
    for part in PARTS:
        arrived(part, 0)
        here, got, held = own(part), bufs[part][0], bufs[part][1]

        @pl.loop(0, 16)
        def _(n, here=here, got=got, held=held):
            a, b = lax.div(n, 4), lax.rem(n, 4)
            value = here(a, b)[...].astype(jnp.float32)
            for step in range(3):
                value += got[step, a, b].astype(jnp.float32)
            held[a, b] = value.astype(jnp.bfloat16)

        launch(part, 1, lambda at, part=part: second(part, at))
    for part in PARTS:
        arrived(part, 1)
        here, got, held = second(part, pos[ORDERS[part][1]]), bufs[part][2], bufs[part][3]
        for a in range(4):
            value = here[a].astype(jnp.float32)
            for step in range(3):
                value += got[step, a].astype(jnp.float32)
            held[a] = value.astype(jnp.bfloat16)
        launch(part, 2, lambda at, held=held: held.at[at])
    for part in PARTS:
        arrived(part, 2)
        value = bufs[part][3][pos[ORDERS[part][2]]].astype(jnp.float32)
        for step in range(3):
            value += bufs[part][4][step].astype(jnp.float32)
        total[pl.ds(*CUT_RS[part]), :] = value
    for started in copies.values():
        for copy in started:
            copy.wait_send()


def all_gather(pos, core, blocks, send_sems, recv_sems):
    copies = {}

    def launch(stage):
        for part in PARTS:
            if stage:
                for copy in copies[part, stage - 1]:
                    copy.wait_recv()
            done = ORDERS[part][:stage]
            index = tuple(slice(None) if a in done else pos[a] for a in range(3)) + (pl.ds(*CUT_AG[part]),)
            axis = ORDERS[part][stage]
            copies[part, stage] = []
            for step in (2, 1, 3):
                copy = send(
                    blocks.at[index],
                    blocks.at[index],
                    send_sems.at[part, stage, step - 1],
                    recv_sems.at[part, stage, step - 1],
                    device_at(moved(pos, axis, step), core),
                )
                copy.start()
                copies[part, stage].append(copy)

    def finish():
        for part in PARTS:
            for copy in copies[part, 2]:
                copy.wait_recv()
        for started in copies.values():
            for copy in started:
                copy.wait_send()

    return launch, finish


def gram_sum(pos, core, panel, pieces, got, mine, whole, sems):
    chip = pos[0] * 16 + pos[1] * 4 + pos[2]
    gram = dot(panel, panel, 0, 0, HI)
    pieces[0:32] = gram[:, :SUB].reshape(32, 8, SUB)
    pieces[32:64] = gram[:, SUB:].reshape(32, 8, SUB)

    def peer(step):
        to = lax.rem(chip + step, 64)
        return to, device_at((lax.div(to, 16), lax.rem(lax.div(to, 4), 4), lax.rem(to, 4)), core)

    @pl.loop(1, 64)
    def _(step):
        to, device = peer(step)
        send(pieces.at[to], got.at[step], sems.at[0], sems.at[1], device).start()

    got[0] = pieces[chip]
    everyone = send(pieces.at[pl.ds(1, 63)], got.at[pl.ds(1, 63)], sems.at[0], sems.at[1], peer(1)[1])
    everyone.wait_recv()
    value = jnp.sum(got[...], axis=0)
    mine[...] = value
    whole[chip] = value

    @pl.loop(1, 64)
    def _(step):
        send(mine, whole.at[chip], sems.at[2], sems.at[3], peer(step)[1]).start()

    everyone.wait_send()
    last = send(got.at[pl.ds(1, 63)], whole.at[pl.ds(1, 63)], sems.at[2], sems.at[3], peer(1)[1])
    last.wait_recv()
    last.wait_send()


def kernel(base, adjusted, omega, up, down, *scratch):
    (
        load_base, load_adjusted, load_sems, apart, delta, outgoing, delta_sems, sketch_map, map_sems,
        sketch, sketch_got, power, power_got, panel, swap_sems, turned, source,
        *rest,
    ) = scratch
    bufs = [rest[5 * part : 5 * part + 5] for part in PARTS]
    (
        total, rs_send, rs_recv, slab_sems, columns, ag_send, ag_recv,
        pieces, gram_got, gram_mine, gram, gram_sems, work, factor, spread, spread_send, spread_recv,
    ) = rest[30:]
    row, col = lax.axis_index("row"), lax.axis_index("col")
    core = lax.rem(col, 2)
    pos = (lax.div(col, 4), lax.rem(lax.div(col, 2), 2) * 2 + lax.div(row, 4), lax.rem(row, 4))
    mate = device_at(pos, 1 - core)

    def load(n):
        slot = lax.rem(n, 4)
        block = 2 * lax.rem(n, 8) + jnp.where(n < 8, 1 - core, core)
        copies = []
        for tile in range(4):
            lanes = pl.ds(pl.multiple_of(block * WIDE + tile * SUB, SUB), SUB)
            for which, (array, held) in enumerate(((base, load_base), (adjusted, load_adjusted))):
                copies.append(
                    pltpu.make_async_copy(array.at[:, :, lanes], held.at[slot, tile], load_sems.at[slot, which, tile])
                )
        return copies

    for n in range(4):
        for copy in load(n):
            copy.start()
    eighth = pl.ds(pl.multiple_of(pos[2] * SUB + lax.rem(pos[1], 2) * 64, 64), 64)
    own_map = [
        pltpu.make_async_copy(
            omega.at[m, eighth], sketch_map.at[pos[0], pos[1], pos[2], pl.ds(m * 64, 64)], map_sems.at[m]
        )
        for m in range(2)
    ]
    for copy in own_map:
        copy.start()

    barrier = pltpu.get_barrier_semaphore()
    near = [moved(pos, axis, step) for axis in range(3) for step in (1, 2, 3)]
    for device in [mate] + [device_at(to, core) for to in near]:
        pl.semaphore_signal(barrier, 1, device_id=device, device_id_type=MESH)
    pl.semaphore_wait(barrier, 10)

    launch_map, finish_map = all_gather(pos, core, sketch_map, ag_send, ag_recv)
    for copy in own_map:
        copy.wait()
    launch_map(0)
    zeros = jnp.zeros((2, PAD - 224, WIDE), jnp.bfloat16)

    def subtract(low, high, leaving):
        @pl.loop(low, high)
        def _(n):
            slot = lax.rem(n, 4)
            for copy in load(n):
                copy.wait()
            place = outgoing.at[n] if leaving else delta.at[n - 8, core]
            place[:, 224:, :] = zeros
            for tile in range(4):
                value = load_adjusted[slot, tile].astype(jnp.float32) - load_base[slot, tile].astype(jnp.float32)
                apart[tile, 0 : 2 * ROWS] = value.reshape(2 * ROWS, SUB)
                for m in range(2):
                    rows = apart[tile, pl.ds(m, ROWS, stride=2), :]
                    place[m, 0:ROWS, tile * SUB : (tile + 1) * SUB] = rows.astype(jnp.bfloat16)

            @pl.when(n < 12)
            def _():
                for copy in load(n + 4):
                    copy.start()

            if leaving:
                send(outgoing.at[n], delta.at[n, core], delta_sems.at[0, n], delta_sems.at[1, n], mate).start()

    subtract(0, 3, True)
    launch_map(1)
    subtract(3, 8, True)
    subtract(8, 9, False)
    launch_map(2)
    subtract(9, 16, False)
    for n in range(8):
        send(outgoing.at[n], delta.at[n, core], delta_sems.at[0, n], delta_sems.at[1, n], mate).wait()
    finish_map()

    def swap(part, got, which):
        copy = send(part, got, swap_sems.at[0, which], swap_sems.at[1, which], mate)
        copy.start()
        copy.wait()

    def product(right, part, got, which):
        copies = []
        for order, m in enumerate((1 - core, core)):
            part[m] = jnp.zeros((2 * PAD, RANK), jnp.float32)

            @pl.loop(0, 8)
            def _(i, m=m):
                part[m] += dot(delta[i, :, m].reshape(2 * PAD, WIDE), right(i, m), 1, 0)

            copy = send(part.at[m], got.at[m], swap_sems.at[0, which + order], swap_sems.at[1, which + order], mate)
            copy.start()
            copies.append(copy)
        copies[0].wait_recv()
        panel[core] = part[core] + got[core]

        def finish():
            copies[1].wait_recv()
            panel[1 - core] = part[1 - core] + got[1 - core]
            for copy in copies:
                copy.wait_send()

        return finish

    def folded(between):
        def fill(x):
            @pl.loop(0, 2)
            def _(n):
                for m in range(2):
                    value = dot(turned[m], delta[x * 2 + n, :, m].reshape(2 * PAD, WIDE), 1, 0).astype(jnp.bfloat16)
                    for z in range(4):
                        source[x, n * 2 + m, z] = value[:, z * SUB : (z + 1) * SUB]

        reduce_scatter(pos, core, source, fill, bufs, total, rs_send, rs_recv, slab_sems, between)

    def orthonormal(finish, which):
        gram_sum(pos, core, panel[core], pieces, gram_got, gram_mine, gram, gram_sems)
        finish()
        invert_factor(gram, work, factor.at[core])
        swap(factor.at[core], factor.at[core], which)
        for m in range(2):
            turned[m] = dot(factor[m], panel[m], 1, 1, HI).astype(jnp.bfloat16)

    def sketch_rows(i, m):
        x, yh = lax.div(i, 2), lax.rem(i, 2)
        rows = pl.ds(pl.multiple_of(m * 64, 64), 64)
        return jnp.concatenate(
            [sketch_map[x, yh * 2 + low, z, rows, :] for z in range(4) for low in range(2)], axis=0
        )

    def column_rows(i, m):
        return columns[lax.div(i, 2), lax.rem(i, 2) * 2 + m].reshape(WIDE, RANK)

    orthonormal(product(sketch_rows, sketch, sketch_got, 0), 4)
    folded(lambda: None)
    columns[pos[0], pos[1], pos[2]] = total[...].T.astype(jnp.bfloat16)
    launch, finish_columns = all_gather(pos, core, columns, ag_send, ag_recv)
    for stage in range(3):
        launch(stage)
    finish_columns()
    orthonormal(product(column_rows, power, power_got, 2), 5)

    def adapter_up():
        for m in range(2):
            rows = panel[m, pl.ds(pl.multiple_of(core * PAD, PAD), PAD), :]
            up[:, m, :] = (dot(rows, factor[m], 1, 1, HI) * math.sqrt(29568))[:ROWS]

    folded(adapter_up)

    spread_copies = []
    for step in range(1, 8):
        to = lax.rem(row + step, 8)
        rows = pl.ds(pl.multiple_of(to * 32, 32), 32)
        copy = send(
            total.at[rows],
            spread.at[row],
            spread_send.at[step - 1],
            spread_recv.at[step - 1],
            {"row": to, "col": col},
        )
        copy.start()
        spread_copies.append(copy)
    spread[row] = total[pl.ds(pl.multiple_of(row * 32, 32), 32), :]
    for copy in spread_copies:
        copy.wait()
    for n in range(8):
        down[n // 4, :, (n % 4) * SUB : (n % 4 + 1) * SUB] = spread[n]


def scratch_shapes():
    half, full = jnp.bfloat16, jnp.float32
    dma = pltpu.SemaphoreType.DMA
    parts = []
    for _, size in CUT_RS:
        parts += [
            pltpu.VMEM((3, 4, 4, size, SUB), half),
            pltpu.VMEM((4, 4, size, SUB), half),
            pltpu.VMEM((3, 4, size, SUB), half),
            pltpu.VMEM((4, size, SUB), half),
            pltpu.VMEM((3, size, SUB), half),
        ]
    return [
        pltpu.VMEM((4, 4, ROWS, 2, SUB), half),
        pltpu.VMEM((4, 4, ROWS, 2, SUB), half),
        dma((4, 2, 4)),
        pltpu.VMEM((4, 2 * PAD, SUB), full),
        pltpu.VMEM((8, 2, 2, PAD, WIDE), half),
        pltpu.VMEM((8, 2, PAD, WIDE), half),
        dma((2, 8)),
        pltpu.VMEM((4, 4, 4, SUB, RANK), half),
        dma((2,)),
        pltpu.VMEM((2, 2 * PAD, RANK), full),
        pltpu.VMEM((2, 2 * PAD, RANK), full),
        pltpu.VMEM((2, 2 * PAD, RANK), full),
        pltpu.VMEM((2, 2 * PAD, RANK), full),
        pltpu.VMEM((2, 2 * PAD, RANK), full),
        dma((2, 6)),
        pltpu.VMEM((2, RANK, 2 * PAD), half),
        pltpu.VMEM((4, 4, 4, RANK, SUB), half),
        *parts,
        pltpu.VMEM((RANK, SUB), full),
        dma((6, 3, 3)),
        dma((6, 3, 3)),
        dma((2, 6, 4, 3)),
        pltpu.VMEM((4, 4, 4, SUB, RANK), half),
        dma((6, 3, 3)),
        dma((6, 3, 3)),
        pltpu.VMEM((64, 8, SUB), full),
        pltpu.VMEM((64, 8, SUB), full),
        pltpu.VMEM((8, SUB), full),
        pltpu.VMEM((64, 8, SUB), full),
        dma((4,)),
        pltpu.VMEM((SUB, 2 * SUB), full),
        pltpu.VMEM((2, RANK, RANK), full),
        pltpu.VMEM((8, 32, SUB), full),
        dma((7,)),
        dma((7,)),
    ]


def local(base_flat, adjusted_flat, omega):
    anywhere = pl.BlockSpec(memory_space=pl.ANY)
    vmem = pl.BlockSpec(memory_space=pltpu.VMEM)
    up, down = pl.pallas_call(
        kernel,
        out_shape=(
            jax.ShapeDtypeStruct((ROWS, 2, RANK), jnp.float32),
            jax.ShapeDtypeStruct((2, 32, WIDE), jnp.float32),
        ),
        in_specs=[anywhere] * 3,
        out_specs=(vmem, vmem),
        scratch_shapes=scratch_shapes(),
        compiler_params=pltpu.CompilerParams(
            collective_id=0, has_side_effects=True, vmem_limit_bytes=60 * 2**20
        ),
    )(base_flat.transpose(1, 0, 2), adjusted_flat.transpose(1, 0, 2), omega)
    return up.transpose(1, 0, 2), down.transpose(0, 2, 1)


def solution(mesh):
    in_specs = (P(None, ("row", "col"), None), P(None, ("row", "col"), None), P(None, "col", None))
    out_specs = (P(None, ("row", "col"), None), P(None, "col", "row"))
    return jax.shard_map(local, mesh=mesh, in_specs=in_specs, out_specs=out_specs, check_vma=False)
```

```python
import math

import jax
import jax.numpy as jnp
from jax import lax
from jax.experimental import pallas as pl
from jax.experimental.pallas import tpu as pltpu
from jax.sharding import PartitionSpec as P

HI = lax.Precision.HIGHEST
MESH = pl.DeviceIdType.MESH
NB = 16
ROWS, PAD, WIDE, RANK, SUB = 231, 240, 512, 256, 128
ORDERS = ((0, 1, 2), (1, 2, 0), (2, 0, 1)) * 2
CUT_RS = ((0, 48), (48, 32), (80, 48), (128, 48), (176, 48), (224, 32))
CUT_AG = ((0, 16), (16, 16), (32, 16), (48, 32), (80, 32), (112, 16))
PARTS = range(6)


def dot(a, b, ca, cb, precision=None):
    return lax.dot_general(a, b, (((ca,), (cb,)), ((), ())), precision=precision, preferred_element_type=jnp.float32)

def terms(value):
    high = value.astype(jnp.bfloat16)
    rest = value - high.astype(jnp.float32)
    middle = rest.astype(jnp.bfloat16)
    return high, middle, (rest - middle.astype(jnp.float32)).astype(jnp.bfloat16)


def factor_panel(work):
    size = 128
    sub = lax.broadcasted_iota(jnp.int32, (NB, size), 0)

    def wide(row):
        return jnp.broadcast_to(row, (NB, size))

    def step(k, carry):
        start = pl.multiple_of(k * NB, NB)
        left, right = work[pl.ds(start, NB), :size], work[pl.ds(start, NB), size:]
        block = pltpu.roll(left, lax.rem(size - start, size), 1)
        cols = [wide(block[:, j : j + 1]) for j in range(NB)]
        diag = cols[0]
        for j in range(NB - 1):
            mult = jnp.where(sub > j, cols[j] * wide(1.0 / cols[j][j : j + 1, :]), 0.0)
            for n in range(j + 1, NB):
                cols[n] = cols[n] - mult * wide(cols[n][j : j + 1, :])
            left = left - mult * wide(left[j : j + 1, :])
            right = right - mult * wide(right[j : j + 1, :])
            diag = jnp.where(sub > j, cols[j + 1], diag)
        scale = lax.rsqrt(diag)
        left, right = left * scale, right * scale
        new = jnp.concatenate([left, right], axis=1)
        high, middle, low = terms(new)
        ahead = jnp.where(lax.broadcasted_iota(jnp.int32, (6 * NB, size), 1) >= start + NB, 1.0, 0.0).astype(jnp.bfloat16)
        below = jnp.concatenate([t[:, :size] for t in (high, high, middle, high, low, middle)], axis=0) * ahead
        other = jnp.concatenate([high, middle, high, low, high, middle], axis=0)
        work[...] -= dot(below, other, 0, 0)
        work[pl.ds(start, NB), :] = new
        return carry
    lax.fori_loop(0, size // NB, step, 0)

def invert_factor(gram, work, out):
    size = 128
    eye = (lax.broadcasted_iota(jnp.int32, (size, size), 0) == lax.broadcasted_iota(jnp.int32, (size, size), 1)).astype(jnp.float32)
    work[:, :size] = gram[0:16].reshape(size, size)
    work[:, size:] = eye
    factor_panel(work)
    t11 = work[:, size:]
    l21 = dot(gram[16:32].reshape(size, size), t11, 1, 1, HI)
    out[:size, :size] = t11
    out[:size, size:] = jnp.zeros((size, size), jnp.float32)
    out[size:, :size] = dot(l21, t11, 1, 0, HI)
    work[:, :size] = gram[48:64].reshape(size, size) - dot(l21, l21, 1, 1, HI)
    work[:, size:] = eye
    factor_panel(work)
    t22 = work[:, size:]
    out[size:, :size] = -dot(t22, out[size:, :size], 1, 0, HI)
    out[size:, size:] = t22


def device_at(pos, core):
    x, y, z = pos
    return {"row": lax.rem(y, 2) * 4 + z, "col": x * 4 + lax.div(y, 2) * 2 + core}


def moved(pos, axis, step):
    return tuple(lax.rem(p + step, 4) if a == axis else p for a, p in enumerate(pos))


def send(src, dst, send_sem, recv_sem, device):
    return pltpu.make_async_remote_copy(
        src_ref=src, dst_ref=dst, send_sem=send_sem, recv_sem=recv_sem, device_id=device, device_id_type=MESH
    )


def reduce_scatter(pos, core, source, fill, bufs, total, send_sems, recv_sems, slab_sems, between):
    copies = {(part, 0): [] for part in PARTS}

    def begin(part, stage, src, dst, sem, step):
        copy = send(src, dst, *sem, device_at(moved(pos, ORDERS[part][stage], step), core))
        copy.start()
        copies[part, stage].append(copy)

    def launch(part, stage, block):
        axis = ORDERS[part][stage]
        copies[part, stage] = []
        for step in (2, 1, 3):
            sem = (send_sems.at[part, stage, step - 1], recv_sems.at[part, stage, step - 1])
            begin(part, stage, block(moved(pos, axis, step)[axis]), bufs[part][2 * stage].at[step - 1], sem, step)

    def slab_out(part, slab, x):
        rows = pl.ds(*CUT_RS[part])
        axis = ORDERS[part][0]
        if axis == 0:
            if slab:
                sem = (send_sems.at[part, 0, slab - 1], recv_sems.at[part, 0, slab - 1])
                begin(part, 0, source.at[x, :, :, rows], bufs[part][0].at[slab - 1], sem, slab)
            return
        for step in (2, 1, 3):
            to = moved(pos, axis, step)
            block = source.at[x, to[1], :, rows] if axis == 1 else source.at[x, :, to[2], rows]
            sem = (slab_sems.at[0, part, slab, step - 1], slab_sems.at[1, part, x, step - 1])
            begin(part, 0, block, bufs[part][0].at[step - 1, x], sem, step)

    def own(part):
        rows = pl.ds(*CUT_RS[part])
        return (
            lambda a: source.at[pos[0], a, :, rows],
            lambda a: source.at[a, pos[1], :, rows],
            lambda a: source.at[a, :, pos[2], rows],
        )[ORDERS[part][0]]

    def second(part, at):
        held = bufs[part][1]
        return held.at[:, at] if ORDERS[part][0] == 1 else held.at[at]

    def arrived(part, stage):
        for copy in copies[part, stage]:
            copy.wait_recv()

    slabs = [(slab, lax.rem(pos[0] + slab, 4)) for slab in (2, 1, 3, 0)]
    for slab, x in slabs:
        fill(x)
        for part in range(3):
            slab_out(part, slab, x)
    for slab, x in slabs:
        for part in range(3, 6):
            slab_out(part, slab, x)
    between()
    for part in PARTS:
        arrived(part, 0)
        here, got, held = own(part), bufs[part][0], bufs[part][1]

        @pl.loop(0, 4)
        def _(a, here=here, got=got, held=held):
            value = here(a)[...].astype(jnp.float32)
            for step in range(3):
                value += got[step, a].astype(jnp.float32)
            held[a] = value.astype(jnp.bfloat16)

        launch(part, 1, lambda at, part=part: second(part, at))
    for part in PARTS:
        arrived(part, 1)
        here, got, held = second(part, pos[ORDERS[part][1]]), bufs[part][2], bufs[part][3]
        for a in range(4):
            value = here[a].astype(jnp.float32)
            for step in range(3):
                value += got[step, a].astype(jnp.float32)
            held[a] = value.astype(jnp.bfloat16)
        launch(part, 2, lambda at, held=held: held.at[at])
    for part in PARTS:
        arrived(part, 2)
        value = bufs[part][3][pos[ORDERS[part][2]]].astype(jnp.float32)
        for step in range(3):
            value += bufs[part][4][step].astype(jnp.float32)
        total[pl.ds(*CUT_RS[part]), :] = value
    for started in copies.values():
        for copy in started:
            copy.wait_send()


def all_gather(pos, core, blocks, send_sems, recv_sems):
    copies = {}

    def launch(stage):
        for part in PARTS:
            if stage:
                for copy in copies[part, stage - 1]:
                    copy.wait_recv()
            done = ORDERS[part][:stage]
            index = tuple(slice(None) if a in done else pos[a] for a in range(3)) + (pl.ds(*CUT_AG[part]),)
            copies[part, stage] = []
            for step in (2, 1, 3) if stage < 2 else (1, 3):
                push(part, stage, step, index, step - 1)

    def push(part, stage, step, index, sem):
        copy = send(
            blocks.at[index],
            blocks.at[index],
            send_sems.at[part, stage, sem],
            recv_sems.at[part, stage, sem],
            device_at(moved(pos, ORDERS[part][stage], step), core),
        )
        copy.start()
        copies[part, stage].append(copy)

    def finish():
        for part in PARTS:
            first, _, axis = ORDERS[part]
            for arrived in tuple(copies[part, 2]):
                arrived.wait_recv()
            for step, half, sem in ((1, 0, 1), (3, 2, 3)):
                behind = lax.rem(pos[axis] + 4 - step, 4)
                index = tuple(
                    behind if a == axis else pl.ds(half, 2) if a == first else slice(None) for a in range(3)
                ) + (pl.ds(*CUT_AG[part]),)
                push(part, 2, step, index, sem)
        for part in PARTS:
            for copy in copies[part, 2][2:]:
                copy.wait_recv()
        for started in copies.values():
            for copy in started:
                copy.wait_send()

    return launch, finish


def gram_sum(pos, core, panel, pieces, got, mine, whole, sems):
    chip = pos[0] * 16 + pos[1] * 4 + pos[2]
    gram = dot(panel, panel, 0, 0, HI)
    pieces[0:32] = gram[:, :SUB].reshape(32, 8, SUB)
    pieces[32:64] = gram[:, SUB:].reshape(32, 8, SUB)

    def peer(step):
        to = lax.rem(chip + step, 64)
        return to, device_at((lax.div(to, 16), lax.rem(lax.div(to, 4), 4), lax.rem(to, 4)), core)

    @pl.loop(1, 64)
    def _(step):
        to, device = peer(step)
        send(pieces.at[to], got.at[step], sems.at[0], sems.at[1], device).start()

    got[0] = pieces[chip]
    everyone = send(pieces.at[pl.ds(1, 63)], got.at[pl.ds(1, 63)], sems.at[0], sems.at[1], peer(1)[1])
    everyone.wait_recv()
    value = jnp.sum(got[...], axis=0)
    mine[...] = value
    whole[chip] = value

    @pl.loop(1, 64)
    def _(step):
        send(mine, whole.at[chip], sems.at[2], sems.at[3], peer(step)[1]).start()

    everyone.wait_send()
    last = send(got.at[pl.ds(1, 63)], whole.at[pl.ds(1, 63)], sems.at[2], sems.at[3], peer(1)[1])
    last.wait_recv()
    last.wait_send()


def kernel(base, adjusted, omega, up, down, *scratch):
    (
        load_base, load_adjusted, load_sems, apart, delta, outgoing, delta_sems, sketch_map, map_sems,
        sketch, sketch_got, power, power_got, panel, swap_sems, turned, source,
        *rest,
    ) = scratch
    bufs = [rest[5 * part : 5 * part + 5] for part in PARTS]
    (
        total, rs_send, rs_recv, slab_sems, columns, ag_send, ag_recv,
        pieces, gram_got, gram_mine, gram, gram_sems, work, factor, spread, spread_send, spread_recv,
    ) = rest[30:]
    row, col = lax.axis_index("row"), lax.axis_index("col")
    core = lax.rem(col, 2)
    pos = (lax.div(col, 4), lax.rem(lax.div(col, 2), 2) * 2 + lax.div(row, 4), lax.rem(row, 4))
    mate = device_at(pos, 1 - core)

    def load(n):
        slot = lax.rem(n, 4)
        block = 2 * lax.rem(n, 8) + jnp.where(n < 8, 1 - core, core)
        copies = []
        for tile in range(4):
            lanes = pl.ds(pl.multiple_of(block * WIDE + tile * SUB, SUB), SUB)
            for which, (array, held) in enumerate(((base, load_base), (adjusted, load_adjusted))):
                copies.append(
                    pltpu.make_async_copy(array.at[:, :, lanes], held.at[slot, tile], load_sems.at[slot, which, tile])
                )
        return copies

    for n in range(4):
        for copy in load(n):
            copy.start()
    eighth = pl.ds(pl.multiple_of(pos[2] * SUB + lax.rem(pos[1], 2) * 64, 64), 64)
    own_map = [
        pltpu.make_async_copy(
            omega.at[m, eighth], sketch_map.at[pos[0], pos[1], pos[2], pl.ds(m * 64, 64)], map_sems.at[m]
        )
        for m in range(2)
    ]
    for copy in own_map:
        copy.start()

    barrier = pltpu.get_barrier_semaphore()
    near = [moved(pos, axis, step) for axis in range(3) for step in (1, 2, 3)]
    for device in [mate] + [device_at(to, core) for to in near]:
        pl.semaphore_signal(barrier, 1, device_id=device, device_id_type=MESH)
    pl.semaphore_wait(barrier, 10)

    launch_map, finish_map = all_gather(pos, core, sketch_map, ag_send, ag_recv)
    for copy in own_map:
        copy.wait()
    launch_map(0)
    zeros = jnp.zeros((2, PAD - 224, WIDE), jnp.bfloat16)

    def subtract(low, high, leaving):
        @pl.loop(low, high)
        def _(n):
            slot = lax.rem(n, 4)
            for copy in load(n):
                copy.wait()
            place = outgoing.at[n] if leaving else delta.at[n - 8, core]
            place[:, 224:, :] = zeros
            for tile in range(4):
                value = load_adjusted[slot, tile].astype(jnp.float32) - load_base[slot, tile].astype(jnp.float32)
                apart[tile, 0 : 2 * ROWS] = value.reshape(2 * ROWS, SUB)
                for m in range(2):
                    rows = apart[tile, pl.ds(m, ROWS, stride=2), :]
                    place[m, 0:ROWS, tile * SUB : (tile + 1) * SUB] = rows.astype(jnp.bfloat16)

            @pl.when(n < 12)
            def _():
                for copy in load(n + 4):
                    copy.start()

            if leaving:
                send(outgoing.at[n], delta.at[n, core], delta_sems.at[0, n], delta_sems.at[1, n], mate).start()

    subtract(0, 3, True)
    launch_map(1)
    subtract(3, 8, True)
    subtract(8, 9, False)
    launch_map(2)
    subtract(9, 16, False)
    for n in range(8):
        send(outgoing.at[n], delta.at[n, core], delta_sems.at[0, n], delta_sems.at[1, n], mate).wait()
    finish_map()

    def product(right, part, got, which):
        copies = []
        for order, m in enumerate((1 - core, core)):
            part[m] = jnp.zeros((2 * PAD, RANK), jnp.float32)

            @pl.loop(0, 4)
            def _(n, m=m):
                two = [
                    dot(delta[i, :, m].reshape(2 * PAD, WIDE), right(i, m), 1, 0) for i in (2 * n, 2 * n + 1)
                ]
                part[m] += two[0] + two[1]

            copy = send(part.at[m], got.at[m], swap_sems.at[0, which + order], swap_sems.at[1, which + order], mate)
            copy.start()
            copies.append(copy)
        copies[0].wait_recv()
        panel[core] = part[core] + got[core]

        def finish():
            copies[1].wait_recv()
            panel[1 - core] = part[1 - core] + got[1 - core]
            for copy in copies:
                copy.wait_send()

        return finish

    def folded(between):
        def fill(x):
            @pl.loop(0, 2)
            def _(n):
                for m in range(2):
                    value = dot(turned[m], delta[x * 2 + n, :, m].reshape(2 * PAD, WIDE), 1, 0).astype(jnp.bfloat16)
                    for z in range(4):
                        source[x, n * 2 + m, z] = value[:, z * SUB : (z + 1) * SUB]

        reduce_scatter(pos, core, source, fill, bufs, total, rs_send, rs_recv, slab_sems, between)

    def orthonormal(finish, which):
        gram_sum(pos, core, panel[core], pieces, gram_got, gram_mine, gram, gram_sems)
        finish()
        invert_factor(gram, work, factor.at[core])
        copy = send(factor.at[core], factor.at[core], swap_sems.at[0, which], swap_sems.at[1, which], mate)
        copy.start()
        turned[core] = dot(factor[core], panel[core], 1, 1, HI).astype(jnp.bfloat16)
        copy.wait()
        turned[1 - core] = dot(factor[1 - core], panel[1 - core], 1, 1, HI).astype(jnp.bfloat16)

    def sketch_rows(i, m):
        x, yh = lax.div(i, 2), lax.rem(i, 2)
        rows = pl.ds(pl.multiple_of(m * 64, 64), 64)
        return jnp.concatenate(
            [sketch_map[x, yh * 2 + low, z, rows, :] for z in range(4) for low in range(2)], axis=0
        )

    def column_rows(i, m):
        return columns[lax.div(i, 2), lax.rem(i, 2) * 2 + m].reshape(WIDE, RANK)

    orthonormal(product(sketch_rows, sketch, sketch_got, 0), 4)
    folded(lambda: None)
    columns[pos[0], pos[1], pos[2]] = total[...].T.astype(jnp.bfloat16)
    launch, finish_columns = all_gather(pos, core, columns, ag_send, ag_recv)
    for stage in range(3):
        launch(stage)
    finish_columns()
    orthonormal(product(column_rows, power, power_got, 2), 5)

    def adapter_up():
        for m in range(2):
            rows = panel[m, pl.ds(pl.multiple_of(core * PAD, PAD), PAD), :]
            up[:, m, :] = (dot(rows, factor[m], 1, 1, HI) * math.sqrt(29568))[:ROWS]

    folded(adapter_up)

    spread_copies = []
    for step in range(1, 8):
        to = lax.rem(row + step, 8)
        rows = pl.ds(pl.multiple_of(to * 32, 32), 32)
        copy = send(
            total.at[rows],
            spread.at[row],
            spread_send.at[step - 1],
            spread_recv.at[step - 1],
            {"row": to, "col": col},
        )
        copy.start()
        spread_copies.append(copy)
    spread[row] = total[pl.ds(pl.multiple_of(row * 32, 32), 32), :]
    for copy in spread_copies:
        copy.wait()
    for n in range(8):
        down[n // 4, :, (n % 4) * SUB : (n % 4 + 1) * SUB] = spread[n]


def scratch_shapes():
    half, full = jnp.bfloat16, jnp.float32
    dma = pltpu.SemaphoreType.DMA
    parts = []
    for _, size in CUT_RS:
        parts += [
            pltpu.VMEM((3, 4, 4, size, SUB), half),
            pltpu.VMEM((4, 4, size, SUB), half),
            pltpu.VMEM((3, 4, size, SUB), half),
            pltpu.VMEM((4, size, SUB), half),
            pltpu.VMEM((3, size, SUB), half),
        ]
    return [
        pltpu.VMEM((4, 4, ROWS, 2, SUB), half),
        pltpu.VMEM((4, 4, ROWS, 2, SUB), half),
        dma((4, 2, 4)),
        pltpu.VMEM((4, 2 * PAD, SUB), full),
        pltpu.VMEM((8, 2, 2, PAD, WIDE), half),
        pltpu.VMEM((8, 2, PAD, WIDE), half),
        dma((2, 8)),
        pltpu.VMEM((4, 4, 4, SUB, RANK), half),
        dma((2,)),
        pltpu.VMEM((2, 2 * PAD, RANK), full),
        pltpu.VMEM((2, 2 * PAD, RANK), full),
        pltpu.VMEM((2, 2 * PAD, RANK), full),
        pltpu.VMEM((2, 2 * PAD, RANK), full),
        pltpu.VMEM((2, 2 * PAD, RANK), full),
        dma((2, 6)),
        pltpu.VMEM((2, RANK, 2 * PAD), half),
        pltpu.VMEM((4, 4, 4, RANK, SUB), half),
        *parts,
        pltpu.VMEM((RANK, SUB), full),
        dma((6, 3, 3)),
        dma((6, 3, 3)),
        dma((2, 6, 4, 3)),
        pltpu.VMEM((4, 4, 4, SUB, RANK), half),
        dma((6, 3, 4)),
        dma((6, 3, 4)),
        pltpu.VMEM((64, 8, SUB), full),
        pltpu.VMEM((64, 8, SUB), full),
        pltpu.VMEM((8, SUB), full),
        pltpu.VMEM((64, 8, SUB), full),
        dma((4,)),
        pltpu.VMEM((SUB, 2 * SUB), full),
        pltpu.VMEM((2, RANK, RANK), full),
        pltpu.VMEM((8, 32, SUB), full),
        dma((7,)),
        dma((7,)),
    ]


def local(base_flat, adjusted_flat, omega):
    anywhere = pl.BlockSpec(memory_space=pl.ANY)
    vmem = pl.BlockSpec(memory_space=pltpu.VMEM)
    up, down = pl.pallas_call(
        kernel,
        out_shape=(
            jax.ShapeDtypeStruct((ROWS, 2, RANK), jnp.float32),
            jax.ShapeDtypeStruct((2, 32, WIDE), jnp.float32),
        ),
        in_specs=[anywhere] * 3,
        out_specs=(vmem, vmem),
        scratch_shapes=scratch_shapes(),
        compiler_params=pltpu.CompilerParams(
            collective_id=0, has_side_effects=True, vmem_limit_bytes=60 * 2**20
        ),
    )(base_flat.transpose(1, 0, 2), adjusted_flat.transpose(1, 0, 2), omega)
    return up.transpose(1, 0, 2), down.transpose(0, 2, 1)


def solution(mesh):
    in_specs = (P(None, ("row", "col"), None), P(None, ("row", "col"), None), P(None, "col", None))
    out_specs = (P(None, ("row", "col"), None), P(None, "col", "row"))
    return jax.shard_map(local, mesh=mesh, in_specs=in_specs, out_specs=out_specs, check_vma=False)
```

```python
import math

import jax
import jax.numpy as jnp
from jax import lax
from jax.experimental import pallas as pl
from jax.experimental.pallas import tpu as pltpu
from jax.sharding import PartitionSpec as P

HI = lax.Precision.HIGHEST
MESH = pl.DeviceIdType.MESH
NB = 16
ROWS, PAD, WIDE, RANK, SUB = 231, 240, 512, 256, 128
ORDERS = ((0, 1, 2), (1, 2, 0), (2, 0, 1)) * 2
CUT_RS = ((0, 48), (48, 32), (80, 48), (128, 48), (176, 48), (224, 32))
CUT_AG = ((0, 16), (16, 16), (32, 16), (48, 32), (80, 32), (112, 16))
PARTS = range(6)


def dot(a, b, ca, cb, precision=None):
    return lax.dot_general(a, b, (((ca,), (cb,)), ((), ())), precision=precision, preferred_element_type=jnp.float32)

def terms(value):
    high = value.astype(jnp.bfloat16)
    rest = value - high.astype(jnp.float32)
    middle = rest.astype(jnp.bfloat16)
    return high, middle, (rest - middle.astype(jnp.float32)).astype(jnp.bfloat16)


def factor_panel(work):
    size = 128
    sub = lax.broadcasted_iota(jnp.int32, (NB, size), 0)

    def wide(row):
        return jnp.broadcast_to(row, (NB, size))

    def step(k, carry):
        start = pl.multiple_of(k * NB, NB)
        left, right = work[pl.ds(start, NB), :size], work[pl.ds(start, NB), size:]
        block = pltpu.roll(left, lax.rem(size - start, size), 1)
        cols = [wide(block[:, j : j + 1]) for j in range(NB)]
        diag = cols[0]
        for j in range(NB - 1):
            mult = jnp.where(sub > j, cols[j] * wide(1.0 / cols[j][j : j + 1, :]), 0.0)
            for n in range(j + 1, NB):
                cols[n] = cols[n] - mult * wide(cols[n][j : j + 1, :])
            left = left - mult * wide(left[j : j + 1, :])
            right = right - mult * wide(right[j : j + 1, :])
            diag = jnp.where(sub > j, cols[j + 1], diag)
        scale = lax.rsqrt(diag)
        left, right = left * scale, right * scale
        new = jnp.concatenate([left, right], axis=1)
        high, middle, low = terms(new)
        ahead = jnp.where(lax.broadcasted_iota(jnp.int32, (6 * NB, size), 1) >= start + NB, 1.0, 0.0).astype(jnp.bfloat16)
        below = jnp.concatenate([t[:, :size] for t in (high, high, middle, high, low, middle)], axis=0) * ahead
        other = jnp.concatenate([high, middle, high, low, high, middle], axis=0)
        work[...] -= dot(below, other, 0, 0)
        work[pl.ds(start, NB), :] = new
        return carry
    lax.fori_loop(0, size // NB, step, 0)

def invert_factor(gram, work, out):
    size = 128
    eye = (lax.broadcasted_iota(jnp.int32, (size, size), 0) == lax.broadcasted_iota(jnp.int32, (size, size), 1)).astype(jnp.float32)
    work[:, :size] = gram[0:16].reshape(size, size)
    work[:, size:] = eye
    factor_panel(work)
    t11 = work[:, size:]
    l21 = dot(gram[16:32].reshape(size, size), t11, 1, 1, HI)
    out[:size, :size] = t11
    out[:size, size:] = jnp.zeros((size, size), jnp.float32)
    out[size:, :size] = dot(l21, t11, 1, 0, HI)
    work[:, :size] = gram[48:64].reshape(size, size) - dot(l21, l21, 1, 1, HI)
    work[:, size:] = eye
    factor_panel(work)
    t22 = work[:, size:]
    out[size:, :size] = -dot(t22, out[size:, :size], 1, 0, HI)
    out[size:, size:] = t22


def device_at(pos, core):
    x, y, z = pos
    return {"row": lax.rem(y, 2) * 4 + z, "col": x * 4 + lax.div(y, 2) * 2 + core}


def moved(pos, axis, step):
    return tuple(lax.rem(p + step, 4) if a == axis else p for a, p in enumerate(pos))


def send(src, dst, send_sem, recv_sem, device):
    return pltpu.make_async_remote_copy(
        src_ref=src, dst_ref=dst, send_sem=send_sem, recv_sem=recv_sem, device_id=device, device_id_type=MESH
    )


def reduce_scatter(pos, core, source, fill, bufs, total, send_sems, recv_sems, slab_sems, between):
    copies = {(part, 0): [] for part in PARTS}

    def begin(part, stage, src, dst, sem, step):
        copy = send(src, dst, *sem, device_at(moved(pos, ORDERS[part][stage], step), core))
        copy.start()
        copies[part, stage].append(copy)

    def launch(part, stage, block):
        axis = ORDERS[part][stage]
        copies[part, stage] = []
        for step in (2, 1, 3):
            sem = (send_sems.at[part, stage, step - 1], recv_sems.at[part, stage, step - 1])
            begin(part, stage, block(moved(pos, axis, step)[axis]), bufs[part][2 * stage].at[step - 1], sem, step)

    def slab_out(part, slab, x):
        rows = pl.ds(*CUT_RS[part])
        axis = ORDERS[part][0]
        if axis == 0:
            if slab:
                sem = (send_sems.at[part, 0, slab - 1], recv_sems.at[part, 0, slab - 1])
                begin(part, 0, source.at[x, :, :, rows], bufs[part][0].at[slab - 1], sem, slab)
            return
        for step in (2, 1, 3):
            to = moved(pos, axis, step)
            block = source.at[x, to[1], :, rows] if axis == 1 else source.at[x, :, to[2], rows]
            sem = (slab_sems.at[0, part, slab, step - 1], slab_sems.at[1, part, x, step - 1])
            begin(part, 0, block, bufs[part][0].at[step - 1, x], sem, step)

    def own(part):
        rows = pl.ds(*CUT_RS[part])
        return (
            lambda a: source.at[pos[0], a, :, rows],
            lambda a: source.at[a, pos[1], :, rows],
            lambda a: source.at[a, :, pos[2], rows],
        )[ORDERS[part][0]]

    def second(part, at):
        held = bufs[part][1]
        return held.at[:, at] if ORDERS[part][0] == 1 else held.at[at]

    def arrived(part, stage):
        for copy in copies[part, stage]:
            copy.wait_recv()

    slabs = [(slab, lax.rem(pos[0] + slab, 4)) for slab in (2, 1, 3, 0)]
    for slab, x in slabs:
        fill(x)
        for part in range(3):
            slab_out(part, slab, x)
    for slab, x in slabs:
        for part in range(3, 6):
            slab_out(part, slab, x)
    between()
    for part in PARTS:
        arrived(part, 0)
        here, got, held = own(part), bufs[part][0], bufs[part][1]

        @pl.loop(0, 4)
        def _(a, here=here, got=got, held=held):
            value = here(a)[...].astype(jnp.float32)
            for step in range(3):
                value += got[step, a].astype(jnp.float32)
            held[a] = value.astype(jnp.bfloat16)

        launch(part, 1, lambda at, part=part: second(part, at))
    for part in PARTS:
        arrived(part, 1)
        here, got, held = second(part, pos[ORDERS[part][1]]), bufs[part][2], bufs[part][3]
        for a in range(4):
            value = here[a].astype(jnp.float32)
            for step in range(3):
                value += got[step, a].astype(jnp.float32)
            held[a] = value.astype(jnp.bfloat16)
        launch(part, 2, lambda at, held=held: held.at[at])
    for part in PARTS:
        arrived(part, 2)
        value = bufs[part][3][pos[ORDERS[part][2]]].astype(jnp.float32)
        for step in range(3):
            value += bufs[part][4][step].astype(jnp.float32)
        total[pl.ds(*CUT_RS[part]), :] = value
    for started in copies.values():
        for copy in started:
            copy.wait_send()


def all_gather(pos, core, blocks, send_sems, recv_sems):
    copies = {}

    def launch(stage):
        for part in PARTS:
            if stage:
                for copy in copies[part, stage - 1]:
                    copy.wait_recv()
            done = ORDERS[part][:stage]
            index = tuple(slice(None) if a in done else pos[a] for a in range(3)) + (pl.ds(*CUT_AG[part]),)
            copies[part, stage] = []
            for step in (2, 1, 3) if stage < 2 else (1, 3):
                push(part, stage, step, index, step - 1)

    def push(part, stage, step, index, sem):
        copy = send(
            blocks.at[index],
            blocks.at[index],
            send_sems.at[part, stage, sem],
            recv_sems.at[part, stage, sem],
            device_at(moved(pos, ORDERS[part][stage], step), core),
        )
        copy.start()
        copies[part, stage].append(copy)

    def finish():
        for part in PARTS:
            first, _, axis = ORDERS[part]
            for arrived in tuple(copies[part, 2]):
                arrived.wait_recv()
            for step, half, sem in ((1, 0, 1), (3, 2, 3)):
                behind = lax.rem(pos[axis] + 4 - step, 4)
                index = tuple(
                    behind if a == axis else pl.ds(half, 2) if a == first else slice(None) for a in range(3)
                ) + (pl.ds(*CUT_AG[part]),)
                push(part, 2, step, index, sem)
        for part in PARTS:
            for copy in copies[part, 2][2:]:
                copy.wait_recv()
        for started in copies.values():
            for copy in started:
                copy.wait_send()

    return launch, finish


def gram_sum(pos, core, panel, pieces, got, mine, whole, sems):
    chip = pos[0] * 16 + pos[1] * 4 + pos[2]
    gram = dot(panel, panel, 0, 0, HI)
    pieces[0:32] = gram[:, :SUB].reshape(32, 8, SUB)
    pieces[32:64] = gram[:, SUB:].reshape(32, 8, SUB)

    def peer(step):
        to = lax.rem(chip + step, 64)
        return to, device_at((lax.div(to, 16), lax.rem(lax.div(to, 4), 4), lax.rem(to, 4)), core)

    @pl.loop(1, 64)
    def _(step):
        to, device = peer(step)
        send(pieces.at[to], got.at[step], sems.at[0], sems.at[1], device).start()

    got[0] = pieces[chip]
    everyone = send(pieces.at[pl.ds(1, 63)], got.at[pl.ds(1, 63)], sems.at[0], sems.at[1], peer(1)[1])
    everyone.wait_recv()
    value = jnp.sum(got[...], axis=0)
    mine[...] = value
    whole[chip] = value

    @pl.loop(1, 64)
    def _(step):
        send(mine, whole.at[chip], sems.at[2], sems.at[3], peer(step)[1]).start()

    everyone.wait_send()
    last = send(got.at[pl.ds(1, 63)], whole.at[pl.ds(1, 63)], sems.at[2], sems.at[3], peer(1)[1])
    last.wait_recv()
    last.wait_send()


def kernel(base, adjusted, omega, up, down, *scratch):
    (
        load_base, load_adjusted, load_sems, apart, delta, outgoing, delta_sems, sketch_map, map_sems,
        sketch, sketch_got, power, power_got, panel, swap_sems, turned, source,
        *rest,
    ) = scratch
    bufs = [rest[5 * part : 5 * part + 5] for part in PARTS]
    (
        total, rs_send, rs_recv, slab_sems, columns, ag_send, ag_recv,
        pieces, gram_got, gram_mine, gram, gram_sems, work, factor, spread, spread_send, spread_recv,
    ) = rest[30:]
    row, col = lax.axis_index("row"), lax.axis_index("col")
    core = lax.rem(col, 2)
    pos = (lax.div(col, 4), lax.rem(lax.div(col, 2), 2) * 2 + lax.div(row, 4), lax.rem(row, 4))
    mate = device_at(pos, 1 - core)

    def load(n):
        slot = lax.rem(n, 4)
        block = 2 * lax.rem(n, 8) + jnp.where(n < 8, 1 - core, core)
        copies = []
        for tile in range(4):
            lanes = pl.ds(pl.multiple_of(block * WIDE + tile * SUB, SUB), SUB)
            for which, (array, held) in enumerate(((base, load_base), (adjusted, load_adjusted))):
                copies.append(
                    pltpu.make_async_copy(array.at[:, :, lanes], held.at[slot, tile], load_sems.at[slot, which, tile])
                )
        return copies

    for n in range(4):
        for copy in load(n):
            copy.start()
    eighth = pl.ds(pl.multiple_of(pos[2] * SUB + lax.rem(pos[1], 2) * 64, 64), 64)
    own_map = [
        pltpu.make_async_copy(
            omega.at[m, eighth], sketch_map.at[pos[0], pos[1], pos[2], pl.ds(m * 64, 64)], map_sems.at[m]
        )
        for m in range(2)
    ]
    for copy in own_map:
        copy.start()

    barrier = pltpu.get_barrier_semaphore()
    near = [moved(pos, axis, step) for axis in range(3) for step in (1, 2, 3)]
    for device in [mate] + [device_at(to, core) for to in near]:
        pl.semaphore_signal(barrier, 1, device_id=device, device_id_type=MESH)
    pl.semaphore_wait(barrier, 10)

    launch_map, finish_map = all_gather(pos, core, sketch_map, ag_send, ag_recv)
    for copy in own_map:
        copy.wait()
    launch_map(0)
    zeros = jnp.zeros((2, PAD - 224, WIDE), jnp.bfloat16)

    def subtract(low, high, leaving):
        @pl.loop(low, high)
        def _(n):
            slot = lax.rem(n, 4)
            for copy in load(n):
                copy.wait()
            place = outgoing.at[n] if leaving else delta.at[n - 8, core]
            place[:, 224:, :] = zeros
            for tile in range(4):
                value = load_adjusted[slot, tile].astype(jnp.float32) - load_base[slot, tile].astype(jnp.float32)
                apart[tile, 0 : 2 * ROWS] = value.reshape(2 * ROWS, SUB)
                for m in range(2):
                    rows = apart[tile, pl.ds(m, ROWS, stride=2), :]
                    place[m, 0:ROWS, tile * SUB : (tile + 1) * SUB] = rows.astype(jnp.bfloat16)

            @pl.when(n < 12)
            def _():
                for copy in load(n + 4):
                    copy.start()

            if leaving:
                send(outgoing.at[n], delta.at[n, core], delta_sems.at[0, n], delta_sems.at[1, n], mate).start()

    subtract(0, 2, True)
    launch_map(1)
    subtract(2, 8, True)
    launch_map(2)
    subtract(8, 16, False)
    for n in range(8):
        send(outgoing.at[n], delta.at[n, core], delta_sems.at[0, n], delta_sems.at[1, n], mate).wait()
    finish_map()

    def product(right, part, got, which):
        copies = []
        for order, m in enumerate((1 - core, core)):
            part[m] = jnp.zeros((2 * PAD, RANK), jnp.float32)

            @pl.loop(0, 4)
            def _(n, m=m):
                two = [
                    dot(delta[i, :, m].reshape(2 * PAD, WIDE), right(i, m), 1, 0) for i in (2 * n, 2 * n + 1)
                ]
                part[m] += two[0] + two[1]

            copy = send(part.at[m], got.at[m], swap_sems.at[0, which + order], swap_sems.at[1, which + order], mate)
            copy.start()
            copies.append(copy)
        copies[0].wait_recv()
        panel[core] = part[core] + got[core]

        def finish():
            copies[1].wait_recv()
            panel[1 - core] = part[1 - core] + got[1 - core]
            for copy in copies:
                copy.wait_send()

        return finish

    def folded(between):
        def fill(x):
            @pl.loop(0, 2)
            def _(n):
                for m in range(2):
                    value = dot(turned[m], delta[x * 2 + n, :, m].reshape(2 * PAD, WIDE), 1, 0).astype(jnp.bfloat16)
                    for z in range(4):
                        source[x, n * 2 + m, z] = value[:, z * SUB : (z + 1) * SUB]

        reduce_scatter(pos, core, source, fill, bufs, total, rs_send, rs_recv, slab_sems, between)

    def orthonormal(finish, which):
        gram_sum(pos, core, panel[core], pieces, gram_got, gram_mine, gram, gram_sems)
        finish()
        invert_factor(gram, work, factor.at[core])
        copy = send(factor.at[core], factor.at[core], swap_sems.at[0, which], swap_sems.at[1, which], mate)
        copy.start()
        turned[core] = dot(factor[core], panel[core], 1, 1, HI).astype(jnp.bfloat16)
        copy.wait()
        turned[1 - core] = dot(factor[1 - core], panel[1 - core], 1, 1, HI).astype(jnp.bfloat16)

    def sketch_rows(i, m):
        x, yh = lax.div(i, 2), lax.rem(i, 2)
        rows = pl.ds(pl.multiple_of(m * 64, 64), 64)
        return jnp.concatenate(
            [sketch_map[x, yh * 2 + low, z, rows, :] for z in range(4) for low in range(2)], axis=0
        )

    def column_rows(i, m):
        return columns[lax.div(i, 2), lax.rem(i, 2) * 2 + m].reshape(WIDE, RANK)

    orthonormal(product(sketch_rows, sketch, sketch_got, 0), 4)
    folded(lambda: None)
    columns[pos[0], pos[1], pos[2]] = total[...].T.astype(jnp.bfloat16)
    launch, finish_columns = all_gather(pos, core, columns, ag_send, ag_recv)
    for stage in range(3):
        launch(stage)
    finish_columns()
    orthonormal(product(column_rows, power, power_got, 2), 5)

    def adapter_up():
        for m in range(2):
            rows = panel[m, pl.ds(pl.multiple_of(core * PAD, PAD), PAD), :]
            up[:, m, :] = (dot(rows, factor[m], 1, 1, HI) * math.sqrt(29568))[:ROWS]

    folded(adapter_up)

    spread_copies = []
    for step in range(1, 8):
        to = lax.rem(row + step, 8)
        rows = pl.ds(pl.multiple_of(to * 32, 32), 32)
        copy = send(
            total.at[rows],
            spread.at[row],
            spread_send.at[step - 1],
            spread_recv.at[step - 1],
            {"row": to, "col": col},
        )
        copy.start()
        spread_copies.append(copy)
    spread[row] = total[pl.ds(pl.multiple_of(row * 32, 32), 32), :]
    for copy in spread_copies:
        copy.wait()
    for n in range(8):
        down[n // 4, :, (n % 4) * SUB : (n % 4 + 1) * SUB] = spread[n]


def scratch_shapes():
    half, full = jnp.bfloat16, jnp.float32
    dma = pltpu.SemaphoreType.DMA
    parts = []
    for _, size in CUT_RS:
        parts += [
            pltpu.VMEM((3, 4, 4, size, SUB), half),
            pltpu.VMEM((4, 4, size, SUB), half),
            pltpu.VMEM((3, 4, size, SUB), half),
            pltpu.VMEM((4, size, SUB), half),
            pltpu.VMEM((3, size, SUB), half),
        ]
    return [
        pltpu.VMEM((4, 4, ROWS, 2, SUB), half),
        pltpu.VMEM((4, 4, ROWS, 2, SUB), half),
        dma((4, 2, 4)),
        pltpu.VMEM((4, 2 * PAD, SUB), full),
        pltpu.VMEM((8, 2, 2, PAD, WIDE), half),
        pltpu.VMEM((8, 2, PAD, WIDE), half),
        dma((2, 8)),
        pltpu.VMEM((4, 4, 4, SUB, RANK), half),
        dma((2,)),
        pltpu.VMEM((2, 2 * PAD, RANK), full),
        pltpu.VMEM((2, 2 * PAD, RANK), full),
        pltpu.VMEM((2, 2 * PAD, RANK), full),
        pltpu.VMEM((2, 2 * PAD, RANK), full),
        pltpu.VMEM((2, 2 * PAD, RANK), full),
        dma((2, 6)),
        pltpu.VMEM((2, RANK, 2 * PAD), half),
        pltpu.VMEM((4, 4, 4, RANK, SUB), half),
        *parts,
        pltpu.VMEM((RANK, SUB), full),
        dma((6, 3, 3)),
        dma((6, 3, 3)),
        dma((2, 6, 4, 3)),
        pltpu.VMEM((4, 4, 4, SUB, RANK), half),
        dma((6, 3, 4)),
        dma((6, 3, 4)),
        pltpu.VMEM((64, 8, SUB), full),
        pltpu.VMEM((64, 8, SUB), full),
        pltpu.VMEM((8, SUB), full),
        pltpu.VMEM((64, 8, SUB), full),
        dma((4,)),
        pltpu.VMEM((SUB, 2 * SUB), full),
        pltpu.VMEM((2, RANK, RANK), full),
        pltpu.VMEM((8, 32, SUB), full),
        dma((7,)),
        dma((7,)),
    ]


def local(base_flat, adjusted_flat, omega):
    anywhere = pl.BlockSpec(memory_space=pl.ANY)
    vmem = pl.BlockSpec(memory_space=pltpu.VMEM)
    up, down = pl.pallas_call(
        kernel,
        out_shape=(
            jax.ShapeDtypeStruct((ROWS, 2, RANK), jnp.float32),
            jax.ShapeDtypeStruct((2, 32, WIDE), jnp.float32),
        ),
        in_specs=[anywhere] * 3,
        out_specs=(vmem, vmem),
        scratch_shapes=scratch_shapes(),
        compiler_params=pltpu.CompilerParams(
            collective_id=0, has_side_effects=True, vmem_limit_bytes=60 * 2**20
        ),
    )(base_flat.transpose(1, 0, 2), adjusted_flat.transpose(1, 0, 2), omega)
    return up.transpose(1, 0, 2), down.transpose(0, 2, 1)


def solution(mesh):
    in_specs = (P(None, ("row", "col"), None), P(None, ("row", "col"), None), P(None, "col", None))
    out_specs = (P(None, ("row", "col"), None), P(None, "col", "row"))
    return jax.shard_map(local, mesh=mesh, in_specs=in_specs, out_specs=out_specs, check_vma=False)
```
